128 devices in a mesh: seq: 32 (over z, x_hi, y), mp: 4 (over x_lo, core).
Axes of the slice: x: 4 (x_hi: 2, x_lo: 2; x = x_hi * 2 + x_lo), y: 4, z: 4, core: 2. Of those that a mesh axis runs over, the one named last changes fastest.
Arguments:
- ids: int32 [4096], P('seq'), may hold values from 0 to 3
- hidden_fwd: bfloat16 [4096, 1024], P('seq', 'mp'), may hold values from -8 to 8
- hidden_rc: bfloat16 [4096, 1024], P('seq', 'mp'), may hold values from -8 to 8
- embed: float32 [4, 1024], P(None, 'mp'), may hold values from -4 to 4
- ln1_gain: float32 [1024], replicated, may hold values from 0.1 to 1.9
- ln2_gain: float32 [1024], replicated, may hold values from 0.1 to 1.9
- mixing: float32 [5, 1024], replicated, may hold values from 0 to 1
- w_receptance: bfloat16 [1024, 1024], P(None, 'mp'), may hold values from -0.1875 to 0.1875
- w_key: bfloat16 [1024, 1024], P(None, 'mp'), may hold values from -0.1875 to 0.1875
- w_value: bfloat16 [1024, 1024], P(None, 'mp'), may hold values from -0.1875 to 0.1875
- decay_first_weight: bfloat16 [1024, 64], replicated, may hold values from -0.1875 to 0.1875
- decay_base: float32 [1024], P('mp'), may hold values from -11 to 1
- decay_second_weight: bfloat16 [64, 1024], P(None, 'mp'), may hold values from -0.75 to 0.75
- context_rate_first_weight: bfloat16 [1024, 64], replicated, may hold values from -0.1875 to 0.1875
- iclr_base: float32 [1024], P('mp'), may hold values from -9 to 1
- context_rate_second_weight: bfloat16 [64, 1024], P(None, 'mp'), may hold values from -0.75 to 0.75
- group_gain: float32 [1024], P('mp'), may hold values from 0.1 to 1.9
- w_output: bfloat16 [1024, 1024], P('mp'), may hold values from -0.1875 to 0.1875
- ffn_key: bfloat16 [1024, 4096], P(None, 'mp'), may hold values from -0.1875 to 0.1875
- ffn_value: bfloat16 [4096, 1024], P('mp'), may hold values from -0.09375 to 0.09375
Outputs:
- merged: bfloat16 [4096, 1024], P('seq', 'mp')
The draws below stay inside these ranges and needn't reach their ends.
Inputs may be any that keep to these rules, and one draw needn't show every extreme that they name: `ids`: bases A, C, G, T are 0, 1, 2, 3; the complement of base c is 3 - c.
All inputs are finite; a program needn't handle non-finite values.
Results may differ from the reference program's by a relative error of at most 0.01.
Values may be sent and summed in bfloat16 or wider, within the bound.
A program may use at most 64 MiB of HBM per device.

```python
import jax
import jax.numpy as jnp
from jax import lax

MODEL_WIDTH = 1024
HEADS = 16
HEAD = 64
FF = 4096
RANK_WIDTH = 64
LENGTH = 4096


def stream_draw(key, salt):
    base_key = jax.random.fold_in(key, salt)
    noise_key = jax.random.fold_in(base_key, 1)
    rough_key = jax.random.fold_in(base_key, 2)
    column = jnp.arange(MODEL_WIDTH, dtype=jnp.float32) / (MODEL_WIDTH - 1)
    rough = jnp.exp(jax.random.uniform(rough_key, (MODEL_WIDTH,), jnp.float32, -0.2877, 0.2877))
    noise = jnp.clip(jax.random.normal(noise_key, (LENGTH, MODEL_WIDTH), jnp.float32), -3.0, 3.0)
    scales = 0.4 * jnp.exp(jnp.log(5.0) * column) * rough
    centre = -0.6 + 1.5 * column
    values = centre[None, :] + scales[None, :] * noise
    return jnp.clip(values, -8.0, 8.0).astype(jnp.bfloat16)


def draw_hidden_fwd(key, part):
    return stream_draw(key, 101)


def draw_hidden_rc(key, part):
    return stream_draw(key, 202)


def place_ends(drawn, rng, least, largest):
    index_at = [jax.random.randint(jax.random.fold_in(rng, axis), (), 0, length) for axis, length in enumerate(drawn.shape)]
    widest = drawn.shape.index(max(drawn.shape))
    beside = index_at[:widest] + [(index_at[widest] + 1) % drawn.shape[widest]] + index_at[widest + 1:]
    return drawn.at[tuple(index_at)].set(least).at[tuple(beside)].set(largest)


def block_levels(own_key, extent, cuts, least, top_value):
    level, own = 1.0, jax.random.fold_in(own_key, 6)
    for position, shards_of in cuts:
        draws = jnp.exp(jax.random.uniform(jax.random.fold_in(own, position), (shards_of,), jnp.float32, least / len(cuts), top_value / len(cuts)))
        level = level * jnp.repeat(draws, extent[position] // shards_of).reshape([-1 if axis == position else 1 for axis in range(len(extent))])
    return level


def bell_draw(stream_key, shape, deviation, limit, shards=(), kind=jnp.bfloat16):
    loudness = block_levels(stream_key, shape, shards, -0.22, 0.18) if shards else 1.0
    values = jax.random.normal(stream_key, shape, jnp.float32) * deviation * loudness
    return jnp.minimum(jnp.maximum(values, -limit), limit).astype(kind)


def setup_inputs(seed: int = 0) -> dict:
    arg_keys = jax.random.split(jax.random.key(seed), 21)
    ids = place_ends(jax.random.randint(arg_keys[0], (LENGTH,), 0, 4), jax.random.fold_in(arg_keys[0], 1), 0, 3).astype(jnp.int32)
    hidden_fwd = draw_hidden_fwd(jax.random.fold_in(arg_keys[20], 71), 0)
    hidden_rc = draw_hidden_rc(jax.random.fold_in(arg_keys[20], 71), 0)
    embed = bell_draw(arg_keys[3], (4, MODEL_WIDTH), 1.0, 4.0, ((1, 4),), jnp.float32)
    ln1_gain = jnp.clip(1.0 + 0.18 * jax.random.normal(arg_keys[4], (MODEL_WIDTH,), jnp.float32), 0.1, 1.9)
    ln2_gain = jnp.clip(1.0 + 0.18 * jax.random.normal(arg_keys[5], (MODEL_WIDTH,), jnp.float32), 0.1, 1.9)
    mixing = jnp.clip(jax.random.uniform(arg_keys[6], (5, MODEL_WIDTH), jnp.float32, 0.0, 1.0), 0.0, 1.0)
    w_receptance = bell_draw(arg_keys[7], (MODEL_WIDTH, MODEL_WIDTH), MODEL_WIDTH ** -0.5, 0.1875, ((1, 4),))
    w_key = bell_draw(arg_keys[8], (MODEL_WIDTH, MODEL_WIDTH), MODEL_WIDTH ** -0.5, 0.1875, ((1, 4),))
    w_value = bell_draw(arg_keys[9], (MODEL_WIDTH, MODEL_WIDTH), MODEL_WIDTH ** -0.5, 0.1875, ((1, 4),))
    decay_first_weight = bell_draw(arg_keys[10], (MODEL_WIDTH, RANK_WIDTH), MODEL_WIDTH ** -0.5, 0.1875)
    decay_base = jnp.clip(-11.0 + 12.0 * jax.random.uniform(arg_keys[11], (MODEL_WIDTH,), jnp.float32) ** block_levels(arg_keys[11], (MODEL_WIDTH,), ((0, 4),), -0.2, 0.2), -11.0, 1.0)
    decay_second_weight = bell_draw(arg_keys[12], (RANK_WIDTH, MODEL_WIDTH), RANK_WIDTH ** -0.5, 0.75, ((1, 4),))
    context_rate_first_weight = bell_draw(arg_keys[13], (MODEL_WIDTH, RANK_WIDTH), MODEL_WIDTH ** -0.5, 0.1875)
    iclr_base = jnp.clip(-9.0 + 10.0 * jax.random.uniform(arg_keys[14], (MODEL_WIDTH,), jnp.float32) ** block_levels(arg_keys[14], (MODEL_WIDTH,), ((0, 4),), -0.2, 0.2), -9.0, 1.0)
    context_rate_second_weight = bell_draw(arg_keys[15], (RANK_WIDTH, MODEL_WIDTH), RANK_WIDTH ** -0.5, 0.75, ((1, 4),))
    group_gain = jnp.clip(1.0 + 0.18 * jax.random.normal(arg_keys[16], (MODEL_WIDTH,), jnp.float32), 0.1, 1.9)
    w_output = bell_draw(arg_keys[17], (MODEL_WIDTH, MODEL_WIDTH), MODEL_WIDTH ** -0.5, 0.1875, ((0, 4),))
    ffn_key = bell_draw(arg_keys[18], (MODEL_WIDTH, FF), MODEL_WIDTH ** -0.5, 0.1875, ((1, 4),))
    ffn_value = bell_draw(arg_keys[19], (FF, MODEL_WIDTH), FF ** -0.5, 0.09375, ((0, 4),))
    return dict(ids=ids, hidden_fwd=hidden_fwd, hidden_rc=hidden_rc, embed=embed, ln1_gain=ln1_gain, ln2_gain=ln2_gain, mixing=mixing, w_receptance=w_receptance, w_key=w_key, w_value=w_value, decay_first_weight=decay_first_weight, decay_base=decay_base, decay_second_weight=decay_second_weight, context_rate_first_weight=context_rate_first_weight, iclr_base=iclr_base, context_rate_second_weight=context_rate_second_weight, group_gain=group_gain, w_output=w_output, ffn_key=ffn_key, ffn_value=ffn_value)


PRECISE = lax.Precision.HIGHEST
DECAY_SCALE = 0.606531
NORM_EPS = 1e-05
GROUP_EPS = 0.00064
UNIT_EPS = 1e-06

def layer_norm(values, gain):
    row_mean = lax.optimization_barrier(jnp.mean(values, axis=-1, keepdims=True))
    centered = values - row_mean
    spread = lax.optimization_barrier(jnp.mean(centered * centered, axis=-1, keepdims=True))
    return centered * lax.rsqrt(spread + NORM_EPS) * gain

def project(layer_input, weight):
    flat = layer_input.reshape(-1, layer_input.shape[-1])
    result = jnp.dot(flat, weight, preferred_element_type=jnp.float32)
    return result.reshape(layer_input.shape[:-1] + (weight.shape[1],))

def wkv_step(wkv_state, layer_input):
    receptance, decay_rate, key_vec, value_vec, unit_key, iclr_rate = layer_input
    pulled = jnp.einsum('abhvk,abhk->abhv', wkv_state, unit_key, precision=PRECISE)
    wkv_state = wkv_state * decay_rate[..., None, :] - pulled[..., :, None] * (iclr_rate * unit_key)[..., None, :] + value_vec[..., :, None] * key_vec[..., None, :]
    return (wkv_state, jnp.einsum('abhvk,abhk->abhv', wkv_state, receptance, precision=PRECISE))

def timeline(array):
    ordered = jnp.stack([array[0], array[1][:, ::-1]])
    return jnp.moveaxis(ordered, 2, 0)

def reference(ids, hidden_fwd, hidden_rc, embed, ln1_gain, ln2_gain, mixing, w_receptance, w_key, w_value, decay_first_weight, decay_base, decay_second_weight, context_rate_first_weight, iclr_base, context_rate_second_weight, group_gain, w_output, ffn_key, ffn_value):
    letters = jnp.arange(4, dtype=jnp.int32)
    onehot_fwd = (ids[:, None] == letters[None, :]).astype(jnp.float32)
    onehot_rc = ((3 - ids[::-1])[:, None] == letters[None, :]).astype(jnp.float32)
    strands = jnp.stack([hidden_fwd.astype(jnp.float32) + jnp.dot(onehot_fwd, embed, precision=PRECISE), hidden_rc.astype(jnp.float32) + jnp.dot(onehot_rc, embed, precision=PRECISE)]).astype(jnp.bfloat16)
    strands = lax.optimization_barrier(strands)
    normed = layer_norm(strands.astype(jnp.float32), ln1_gain)
    zero_row = jnp.zeros((2, 1, MODEL_WIDTH), jnp.float32)
    before = jnp.concatenate([zero_row, normed[:, :-1]], axis=1)
    after_row = jnp.concatenate([normed[:, 1:], zero_row], axis=1)
    neighbours = jnp.stack([before, after_row])
    center = normed[None]

    def mixed_input(mix_index):
        return (center + (neighbours - center) * mixing[mix_index]).astype(jnp.bfloat16)
    receptance = project(mixed_input(0), w_receptance)
    key_vec = project(mixed_input(1), w_key)
    value_vec = project(mixed_input(2), w_value)
    decay_low = jnp.tanh(project(mixed_input(3), decay_first_weight)).astype(jnp.bfloat16)
    log_decay = -DECAY_SCALE * jax.nn.sigmoid(decay_base + project(decay_low, decay_second_weight))
    iclr_low = project(mixed_input(4), context_rate_first_weight).astype(jnp.bfloat16)
    iclr_rate = jax.nn.sigmoid(iclr_base + project(iclr_low, context_rate_second_weight))
    head_shape = (2, 2, LENGTH, HEADS, HEAD)
    per_head = [array.reshape(head_shape) for array in (receptance, log_decay, key_vec, value_vec, iclr_rate)]
    key_square = lax.optimization_barrier(jnp.sum(per_head[2] * per_head[2], axis=-1, keepdims=True))
    unit_key = per_head[2] * lax.rsqrt(key_square + UNIT_EPS)
    sequence_in = (timeline(per_head[0]), timeline(jnp.exp(per_head[1])), timeline(per_head[2]), timeline(per_head[3]), timeline(unit_key), timeline(per_head[4]))
    start_state = jnp.zeros((2, 2, HEADS, HEAD, HEAD), jnp.float32)
    _, wkv_out = lax.scan(wkv_step, start_state, sequence_in)
    wkv_out = jnp.moveaxis(wkv_out, 0, 2)
    wkv_out = jnp.stack([wkv_out[0], wkv_out[1][:, ::-1]])
    head_mean = lax.optimization_barrier(jnp.mean(wkv_out, axis=-1, keepdims=True))
    centered = wkv_out - head_mean
    head_spread = lax.optimization_barrier(jnp.mean(centered * centered, axis=-1, keepdims=True))
    grouped = (centered * lax.rsqrt(head_spread + GROUP_EPS)).reshape(2, 2, LENGTH, MODEL_WIDTH) * group_gain
    joined = (grouped[0] + grouped[1]).astype(jnp.bfloat16)
    residual = strands.astype(jnp.float32) + project(joined, w_output)
    ffn_in = layer_norm(residual, ln2_gain).astype(jnp.bfloat16)
    activated = jnp.square(jax.nn.relu(project(ffn_in, ffn_key))).astype(jnp.bfloat16)
    strand_out = residual + project(activated, ffn_value)
    rc_final = lax.optimization_barrier(strand_out[1].astype(jnp.bfloat16))
    return (strand_out[0] + rc_final[::-1].astype(jnp.float32)).astype(jnp.bfloat16)
```

```python
import functools

import jax
import jax.numpy as jnp
from jax import lax
from jax.experimental import pallas as pl
from jax.experimental.pallas import tpu as pltpu
from jax.sharding import PartitionSpec as P

F32, BF16 = jnp.float32, jnp.bfloat16
HEAD = 64
ROWS = 128
PAIR = 128
LEVELS = 7
DECAY_SCALE = 0.606531
NORM_EPS = 1e-05
GROUP_EPS = 0.00064
UNIT_EPS = 1e-06
MESH = pl.DeviceIdType.MESH


def dot(a, b):
    return lax.dot_general(a, b, (((1,), (0,)), ((), ())), preferred_element_type=F32)


def dot_t(a, b):
    return lax.dot_general(a, b, (((1,), (1,)), ((), ())), preferred_element_type=F32)


def t_dot(a, b):
    return lax.dot_general(a, b, (((0,), (0,)), ((), ())), preferred_element_type=F32)


def halves(value):
    high = value.astype(BF16)
    return high, (value - high.astype(F32)).astype(BF16)


def iota2(shape, dim):
    return lax.broadcasted_iota(jnp.int32, shape, dim)


def left_half(shape):
    return iota2(shape, 1) % PAIR < HEAD


def layer_norm(values, gain):
    centered = values - jnp.mean(values, axis=-1, keepdims=True)
    spread = jnp.mean(centered * centered, axis=-1, keepdims=True)
    return centered * lax.rsqrt(spread + NORM_EPS) * gain


def masks_into(masks):
    row, col = iota2((ROWS, ROWS), 0), iota2((ROWS, ROWS), 1)
    for level in range(LEVELS):
        size = 1 << level
        same = row // (2 * size) == col // (2 * size)
        row_odd, col_odd = (row // size) % 2, (col // size) % 2
        masks[0, level] = jnp.where(same & (row_odd > col_odd), 1.0, 0.0).astype(BF16)
        masks[1, level] = jnp.where(same & (row_odd < col_odd), 1.0, 0.0).astype(BF16)


def two_heads(value):
    left = left_half(value.shape)
    zero = jnp.zeros_like(value)
    return jnp.concatenate([jnp.where(left, value, zero), jnp.where(left, zero, value)], axis=0)


def packed(value, head):
    half = value.shape[0] // 2
    upper, lower = value[:half], value[half:]
    left = left_half(upper.shape)
    if head == 0:
        return jnp.where(left, upper, pltpu.roll(lower, HEAD, 1))
    return jnp.where(left, pltpu.roll(upper, HEAD, 1), lower)


def unpacked(value):
    return jnp.concatenate([value, pltpu.roll(value, HEAD, 1)], axis=0)


def strand_rows(b, x_tile, idm, embf, st):
    for tile in range(8):
        slot, lanes = tile // 2, pl.ds((tile % 2) * PAIR, PAIR)
        added = embf[slot, 3:4, lanes]
        for letter in range(3):
            added = jnp.where(idm == float(letter), embf[slot, letter : letter + 1, lanes], added)
        st[b, :, tile * PAIR : (tile + 1) * PAIR] = (x_tile(tile) + added).astype(BF16)


def edge_row(piece, index, letter_of, embf, gain, keep):
    row = jnp.concatenate([piece[s].astype(F32)[index : index + 1] for s in range(4)], axis=1)
    letter = jnp.broadcast_to(letter_of, row.shape)
    emb = [jnp.concatenate([embf[s, c : c + 1] for s in range(4)], axis=1) for c in range(4)]
    added = emb[3]
    for c in range(3):
        added = jnp.where(letter == float(c), emb[c], added)
    row = (row + added).astype(BF16).astype(F32)
    return layer_norm(row, gain) * keep


def normed_and_mixed(b, st, nrm, mx, gain, mix):
    for chunk in range(4):
        rows = pl.ds(chunk * 32, 32)
        nrm[8 + chunk * 32 : 40 + chunk * 32] = layer_norm(st[b, rows].astype(F32), gain)
    for chunk in range(8):
        at = chunk * 16
        center = nrm[8 + at : 24 + at]
        before = nrm[7 + at : 23 + at] - center
        after = nrm[9 + at : 25 + at] - center
        for index in range(5):
            weight = mix[index : index + 1, :]
            mx[index, at : at + 16] = (center + before * weight).astype(BF16)
            mx[index, ROWS + at : ROWS + at + 16] = (center + after * weight).astype(BF16)


def projected(mx, wr, wk, wv, dfw, dbase, dsw, cfw, ibase, csw, proj):
    def keep(index, value):
        for beta in range(2):
            for q in range(2):
                proj[index, beta, q] = value[
                    beta * ROWS : (beta + 1) * ROWS, q * PAIR : (q + 1) * PAIR
                ]

    keep(0, dot(mx[0], wr[...]))
    key = dot(mx[1], wk[...])
    keep(1, key)
    keep(2, dot(mx[2], wv[...]))
    width = 2 * PAIR
    same_head = iota2((width, width), 0) // HEAD == iota2((width, width), 1) // HEAD
    ones = jnp.where(same_head, 1.0, 0.0).astype(BF16)
    high, low = halves(key * key)
    square = dot(high, ones) + dot(low, ones)
    keep(3, key * lax.rsqrt(square + UNIT_EPS))
    low_iclr = dot(mx[4], cfw[...]).astype(BF16)
    keep(4, jax.nn.sigmoid(ibase[...] + dot(low_iclr, csw[...])))
    low_decay = jnp.tanh(dot(mx[3], dfw[...])).astype(BF16)
    log_decay = -DECAY_SCALE * jax.nn.sigmoid(dbase[...] + dot(low_decay, dsw[...]))
    keep(5, log_decay)
    row, col = iota2((ROWS, ROWS), 0), iota2((ROWS, ROWS), 1)
    totals = []
    for beta in range(2):
        passed = (row >= col) if beta == 0 else (row <= col)
        ones = jnp.where(passed, 1.0, 0.0).astype(BF16)
        high, low = halves(log_decay[beta * ROWS : (beta + 1) * ROWS])
        totals.append(dot(ones, high) + dot(ones, low))
    keep(6, jnp.concatenate(totals, axis=0))


def block_terms(b, q, proj, masks, msg, aik, uw, vv, srd):
    row, col = iota2((ROWS, ROWS), 0), iota2((ROWS, ROWS), 1)
    eye = jnp.where(row == col, 1.0, 0.0)
    for beta in range(2):
        pair = (beta * 2 + b) * 2 + q
        receptance, key, value, unit, iclr, log_decay, total = [
            proj[i, beta, q] for i in range(7)
        ]
        middle = total[64:65] if beta == 0 else total[63:64]
        final = total[127:128] if beta == 0 else total[0:1]
        scale_here = jnp.exp(total - middle)
        scale_right = jnp.exp(middle - total)
        left_prev = -unit * jnp.exp(total - log_decay - middle)
        left_here = receptance * scale_here
        right_insert = iclr * unit * scale_right
        right_key = key * scale_right
        from_start = jnp.exp(middle)
        to_end = jnp.exp(final - middle)
        left = jnp.concatenate(
            [two_heads(left_prev.astype(BF16)), two_heads(left_here.astype(BF16))], axis=0
        )
        right = jnp.concatenate([right_insert, right_key], axis=0).astype(BF16)
        scores = dot_t(left, right)
        strict = (row > col) if beta == 0 else (row < col)
        inclusive = (row >= col) if beta == 0 else (row <= col)
        inverses = []
        for head in range(2):
            lower = jnp.where(strict, scores[head * ROWS : (head + 1) * ROWS, :ROWS], 0.0)
            lower = lower.astype(BF16)
            inverse = eye + (lower * masks[beta, 0]).astype(F32)
            for level in range(1, LEVELS):
                narrow = inverse.astype(BF16)
                step = dot(narrow, lower * masks[beta, level]).astype(BF16)
                inverse = inverse + dot(step, narrow)
            inverses.append(inverse.astype(BF16))
            at = 2 * ROWS + head * ROWS
            aik[pair, :, head * ROWS : (head + 1) * ROWS] = jnp.where(
                inclusive, scores[at : at + ROWS, :ROWS], 0.0
            ).astype(BF16)
            aik[pair, :, (2 + head) * ROWS : (3 + head) * ROWS] = jnp.where(
                inclusive, scores[at : at + ROWS, ROWS:], 0.0
            ).astype(BF16)
        value = value.astype(BF16)
        vv[pair] = value
        srd[pair] = left_here * from_start
        key_pull = jnp.concatenate(
            [
                jnp.where(strict, scores[head * ROWS : (head + 1) * ROWS, ROWS:], 0.0)
                for head in range(2)
            ],
            axis=1,
        ).astype(BF16)
        pulled = dot(key_pull, two_heads(value))
        wanted = jnp.concatenate([pulled, left_prev * from_start], axis=1).astype(BF16)
        solved = dot(jnp.concatenate(inverses, axis=1), two_heads(wanted)).astype(BF16)
        uw[pair] = solved
        tail_insert = (right_insert * to_end).astype(BF16)
        tail_key = (right_key * to_end).astype(BF16)
        both = t_dot(solved, tail_insert)
        ends = both[:PAIR] + t_dot(value, tail_key)
        moved = both[PAIR:]
        moved = moved + jnp.where(row == col, jnp.exp(final) - 1.0, 0.0)
        left_lanes = left_half((HEAD, PAIR))
        moved = jnp.where(left_lanes, moved[:HEAD], moved[HEAD:])
        ends = jnp.where(left_lanes, ends[:HEAD], ends[HEAD:])
        for head in range(2):
            moved_part = packed(moved, head).astype(BF16)
            for half in range(2):
                unit_at = pair * 4 + head * 2 + half
                msg[unit_at, 0:32] = moved_part
                msg[unit_at, 32:48] = packed(ends[half * 32 : half * 32 + 32], head).astype(BF16)


def local_terms(pair, aik, uw, vv, srd, local, start_map):
    solved = two_heads(uw[pair])
    scores = aik[pair]
    read = dot(scores[:, : 2 * ROWS], solved)
    keyed = dot(scores[:, 2 * ROWS :], two_heads(vv[pair]))
    local[pair] = read[:, :PAIR] + keyed
    start_map[pair] = (srd[pair] + read[:, PAIR:]).astype(BF16)


def scanned(n_seq, backward, recv, ret, inside):
    def place(i):
        return i + backward * (n_seq - 1 - 2 * i)

    size = 4
    groups = n_seq // size
    left = left_half((HEAD + 32, PAIR))
    blank = jnp.zeros((HEAD, PAIR), BF16)

    def block(i):
        value = recv[place(i)].astype(F32)
        whole = jnp.concatenate([unpacked(value[:32]), unpacked(value[32:])], axis=0)
        return jnp.where(left, whole, 0.0)

    def through(state, mapping):
        full = jnp.concatenate([mapping.astype(BF16), blank], axis=0)
        return dot(state.astype(BF16), full)

    for k in range(size):
        for g in range(groups):
            new = block(g * size + k)
            if k:
                so_far = inside[g * size + k - 1]
                new = so_far + new + through(so_far, new[:HEAD])
            inside[g * size + k] = new

    def onward(g, state):
        whole = inside[g * size + size - 1]
        for k in range(size):
            here = state
            if k:
                before = inside[g * size + k - 1]
                here = here + before[HEAD:] + through(here, before[:HEAD])
            ret[place(g * size + k)] = packed(here, 0).astype(BF16)
        return state + whole[HEAD:] + through(state, whole[:HEAD])

    lax.fori_loop(0, groups, onward, jnp.zeros((32, PAIR), F32))


def incoming(pair, states):
    rows = []
    left = left_half((16, PAIR))
    for head in range(2):
        for half in range(2):
            value = states[pair * 4 + head * 2 + half].astype(F32)
            turned = pltpu.roll(value, HEAD, 1)
            if head == 0:
                rows += [jnp.where(left, value, 0.0), jnp.where(left, turned, 0.0)]
            else:
                rows += [jnp.where(left, 0.0, turned), jnp.where(left, 0.0, value)]
    return jnp.concatenate(rows, axis=0).astype(BF16)


def grouped(pair, states, local, start_map, ones):
    out = local[pair] + dot_t(start_map[pair], incoming(pair, states))
    high, low = halves(out)
    centered = out - (dot(high, ones) + dot(low, ones)) * (1.0 / HEAD)
    spread = dot((centered * centered).astype(BF16), ones) * (1.0 / HEAD)
    return centered * lax.rsqrt(spread + GROUP_EPS)


def kernel(
    n_seq, n_mp,
    ids, hidden_fwd, hidden_rc, embed, gain1, gain2, mix,
    w_r, w_k, w_v, d_first, d_base, d_second, c_first, i_base, c_second,
    group_gain, w_out, ffn_key, ffn_value,
    out,
    wr, wk, wv, fk, fv, wo,
    xf, xr, rc_own, embf, prev, nxt, ids_prev, ids_next,
    st, nrm, mx, proj, masks, msg, recv, ret, states, aik, uw, vv, srd, local, start_map,
    joined, residual, act, part, got, inside,
    lsem, ss1, rs1, ss2, rs2, ss3, rs3, ss4, rs4,
):
    j, m = lax.axis_index("seq"), lax.axis_index("mp")

    def seq_at(offset):
        return lax.rem(j + offset + n_seq, n_seq)

    def mp_at(offset):
        return lax.rem(m + offset, n_mp)

    def send(src, dst, sems, index, device):
        copy = pltpu.make_async_remote_copy(
            src_ref=src, dst_ref=dst, send_sem=sems[0].at[index], recv_sem=sems[1].at[index],
            device_id=device, device_id_type=MESH,
        )
        copy.start()
        return copy

    def fetch(src, dst, index):
        copy = pltpu.make_async_copy(src, dst, lsem.at[index])
        copy.start()
        return copy

    barrier = pltpu.get_barrier_semaphore()

    def greet(seq_to, mp_to):
        pl.semaphore_signal(barrier, inc=1, device_id=(seq_to, mp_to), device_id_type=MESH)

    for k in range(1, n_mp):
        greet(j, mp_at(k))
        greet(seq_at(1), mp_at(k))
        greet(seq_at(-1), mp_at(k))

    def greet_far(d, carry):
        greet(seq_at(d), m)
        return carry

    lax.fori_loop(1, n_seq, greet_far, None)

    weights = [
        fetch(src, dst, i)
        for i, (src, dst) in enumerate(
            [(w_r, wr), (w_k, wk), (w_v, wv), (ffn_key, fk), (ffn_value, fv)]
        )
    ]
    own = [
        fetch(hidden_fwd, xf.at[m], 5),
        fetch(embed, embf.at[m], 6),
        fetch(w_out, wo.at[m], 7),
    ]
    masks_into(masks)
    pl.semaphore_wait(barrier, 3 * (n_mp - 1) + n_seq - 1)

    one = (ss1, rs1)
    copies = {}
    copies["mirror"] = send(hidden_rc, rc_own, one, 16, (n_seq - 1 - j, m))
    for k in range(1, n_mp):
        copies["emb", k] = send(embed, embf.at[m], one, 2 + k, (j, mp_at(k)))
        copies["fwd", k] = send(hidden_fwd, xf.at[m], one, k - 1, (j, mp_at(k)))
    for k in range(n_mp):
        copies["f_up", k] = send(
            hidden_fwd.at[pl.ds(ROWS - 16, 16)], prev.at[0, m], one, 6 + k, (seq_at(1), mp_at(k))
        )
        copies["f_down", k] = send(
            hidden_fwd.at[pl.ds(0, 16)], nxt.at[0, m], one, 10 + k, (seq_at(-1), mp_at(k))
        )
    copies["i_up"] = send(ids, ids_prev, one, 14, (seq_at(1), m))
    copies["i_down"] = send(ids, ids_next, one, 15, (seq_at(-1), m))

    letters = jnp.transpose(jnp.broadcast_to(ids[...].astype(F32), (ROWS, ROWS)))
    gain = gain1[...]
    has_prev = (j > 0).astype(F32)
    has_next = (j < n_seq - 1).astype(F32)

    def edges(b):
        sign, base = (1.0, 0.0) if b == 0 else (-1.0, 3.0)
        before = base + sign * ids_prev[0:1, ROWS - 1 : ROWS].astype(F32)
        after = base + sign * ids_next[0:1, 0:1].astype(F32)
        last, first = (15, 0) if b == 0 else (0, 15)
        nrm[7:8] = edge_row(prev.at[b], last, before, embf, gain, has_prev)
        nrm[136:137] = edge_row(nxt.at[b], first, after, embf, gain, has_next)

    def strand(b):
        normed_and_mixed(b, st, nrm, mx, gain, mix)
        projected(mx, wr, wk, wv, d_first, d_base, d_second, c_first, i_base, c_second, proj)

        def body(q, carry):
            block_terms(b, q, proj, masks, msg, aik, uw, vv, srd)
            return carry

        lax.fori_loop(0, 2, body, None)

    copies["mirror"].wait_recv()
    for k in range(1, n_mp):
        copies["rc", k] = send(rc_own, xr.at[m], one, 16 + k, (j, mp_at(k)))
    for k in range(n_mp):
        copies["r_up", k] = send(
            rc_own.at[pl.ds(0, 16)], prev.at[1, m], one, 20 + k, (seq_at(1), mp_at(k))
        )
        copies["r_down", k] = send(
            rc_own.at[pl.ds(ROWS - 16, 16)], nxt.at[1, m], one, 24 + k, (seq_at(-1), mp_at(k))
        )
    own_rc = fetch(rc_own, xr.at[m], 8)
    sibling = m + 1 - 2 * lax.rem(m, 2)
    across = mp_at(2)
    copies["w_near"] = send(w_out, wo.at[m], one, 28, (j, sibling))
    copies["w_far"] = send(w_out, wo.at[m], one, 29, (j, across))

    for copy in own:
        copy.wait()
    for k in range(1, n_mp):
        copies["emb", k].wait_recv()
        copies["fwd", k].wait_recv()
    for k in range(n_mp):
        copies["f_up", k].wait_recv()
        copies["f_down", k].wait_recv()
    copies["i_up"].wait_recv()
    copies["i_down"].wait_recv()
    strand_rows(
        0, lambda t: xf[t // 2, :, (t % 2) * PAIR : (t % 2 + 1) * PAIR].astype(F32),
        letters, embf, st,
    )
    edges(0)
    for copy in weights[:3]:
        copy.wait()
    strand(0)

    own_rc.wait()
    for k in range(1, n_mp):
        copies["rc", k].wait_recv()
    for k in range(n_mp):
        copies["r_up", k].wait_recv()
        copies["r_down", k].wait_recv()
    turn = jnp.where(
        iota2((ROWS, ROWS), 0) + iota2((ROWS, ROWS), 1) == ROWS - 1, 1.0, 0.0
    ).astype(BF16)
    strand_rows(
        1, lambda t: dot(turn, xr[t // 2, :, (t % 2) * PAIR : (t % 2 + 1) * PAIR]),
        3.0 - letters, embf, st,
    )
    edges(1)
    strand(1)

    def to_unit(d):
        return pltpu.make_async_remote_copy(
            src_ref=msg.at[seq_at(d)], dst_ref=recv.at[j],
            send_sem=ss2.at[d], recv_sem=rs2.at[d],
            device_id=(seq_at(d), m), device_id_type=MESH,
        )

    def to_block(d):
        return pltpu.make_async_remote_copy(
            src_ref=ret.at[seq_at(d)], dst_ref=states.at[j],
            send_sem=ss3.at[d], recv_sem=rs3.at[d],
            device_id=(seq_at(d), m), device_id_type=MESH,
        )

    def each(action):
        def body(d, carry):
            action(d)
            return carry

        lax.fori_loop(1, n_seq, body, None)

    each(lambda d: to_unit(d).start())
    own_msg = fetch(msg.at[j], recv.at[j], 9)
    copies["w_far"].wait_recv()
    copies["w_on"] = send(wo.at[across], wo.at[across], one, 30, (j, sibling))

    def local_body(pair, carry):
        local_terms(pair, aik, uw, vv, srd, local, start_map)
        return carry

    lax.fori_loop(0, 8, local_body, None)
    own_msg.wait()
    each(lambda d: to_unit(d).wait_recv())
    scanned(n_seq, j // (n_seq // 2), recv, ret, inside)
    each(lambda d: to_block(d).start())
    own_ret = fetch(ret.at[j], states.at[j], 10)
    own_ret.wait()
    each(lambda d: to_block(d).wait_recv())

    same_head = iota2((PAIR, PAIR), 0) // HEAD == iota2((PAIR, PAIR), 1) // HEAD
    ones = jnp.where(same_head, 1.0, 0.0).astype(BF16)
    four = (ss4, rs4)
    for b in range(2):
        for q in range(2):
            total = grouped(b * 2 + q, states, local, start_map, ones) + grouped(
                4 + b * 2 + q, states, local, start_map, ones
            )
            lanes = slice(q * PAIR, (q + 1) * PAIR)
            joined[m, b * ROWS : (b + 1) * ROWS, lanes] = (
                total * group_gain[:, lanes]
            ).astype(BF16)
        for k in range(1, n_mp):
            block = joined.at[m, pl.ds(b * ROWS, ROWS)]
            copies["join", b, k] = send(block, block, four, b * 3 + k - 1, (j, mp_at(k)))

    copies["w_near"].wait_recv()
    copies["w_on"].wait_recv()
    for copy in weights[3:]:
        copy.wait()
    for b in range(2):
        for k in range(1, n_mp):
            copies["join", b, k].wait_recv()
        rows = slice(b * ROWS, (b + 1) * ROWS)
        whole = st[b].astype(F32)
        for s in range(n_mp):
            whole = whole + dot(joined[s, rows], wo[s])
        residual[rows] = whole
        ffn_in = layer_norm(whole, gain2[...]).astype(BF16)
        act[rows] = jnp.square(jnp.maximum(dot(ffn_in, fk[...]), 0.0)).astype(BF16)

    def partial(index):
        lanes = pl.ds(pl.multiple_of(index * 2 * PAIR, PAIR), 2 * PAIR)
        both = dot(act[...], fv[:, lanes])
        return both[:ROWS] + both[ROWS:], lanes

    for k in range(1, n_mp):
        peer = mp_at(k)
        value, _ = partial(peer)
        part[k - 1] = value.astype(BF16)
        copies["sum", k] = send(part.at[k - 1], got.at[k - 1], four, 5 + k, (j, peer))
    value, lanes = partial(m)
    value = value + residual[:ROWS, lanes] + residual[ROWS:, lanes]
    for k in range(1, n_mp):
        copies["sum", k].wait_recv()
        value = value + got[k - 1].astype(F32)
    out[...] = value.astype(BF16)

    for copy in copies.values():
        copy.wait_send()
    each(lambda d: to_unit(d).wait_send())
    each(lambda d: to_block(d).wait_send())


def on_device(n_seq, n_mp, *args):
    args = list(args)
    args[0] = args[0].reshape(1, ROWS)
    for index in (4, 5, 11, 14, 16):
        args[index] = args[index].reshape(1, -1)
    in_place = {1, 2, 7, 8, 9, 17, 18, 19}
    vmem = pltpu.VMEM
    dma = pltpu.SemaphoreType.DMA
    width = 2 * PAIR
    scratch = [
        vmem((1024, width), BF16), vmem((1024, width), BF16), vmem((1024, width), BF16),
        vmem((1024, 1024), BF16), vmem((1024, 1024), BF16), vmem((n_mp, width, 1024), BF16),
        vmem((n_mp, ROWS, width), BF16), vmem((n_mp, ROWS, width), BF16),
        vmem((ROWS, width), BF16), vmem((n_mp, 4, width), F32),
        vmem((2, n_mp, 16, width), BF16), vmem((2, n_mp, 16, width), BF16),
        vmem((1, ROWS), jnp.int32), vmem((1, ROWS), jnp.int32),
        vmem((2, ROWS, 1024), BF16), vmem((144, 1024), F32), vmem((5, 2 * ROWS, 1024), BF16),
        vmem((7, 2, 2, ROWS, PAIR), F32), vmem((2, LEVELS, ROWS, ROWS), BF16),
        vmem((32, 48, PAIR), BF16), vmem((n_seq, 48, PAIR), BF16),
        vmem((n_seq, 16, PAIR), BF16), vmem((32, 16, PAIR), BF16),
        vmem((8, ROWS, 4 * ROWS), BF16), vmem((8, ROWS, width), BF16),
        vmem((8, ROWS, PAIR), BF16), vmem((8, ROWS, PAIR), F32),
        vmem((8, ROWS, PAIR), F32), vmem((8, ROWS, PAIR), BF16),
        vmem((n_mp, 2 * ROWS, width), BF16), vmem((2 * ROWS, 1024), F32),
        vmem((2 * ROWS, 1024), BF16), vmem((3, ROWS, width), BF16), vmem((3, ROWS, width), BF16),
        vmem((n_seq, 96, PAIR), F32),
        dma((11,)), dma((32,)), dma((32,)), dma((n_seq,)), dma((n_seq,)),
        dma((n_seq,)), dma((n_seq,)), dma((9,)), dma((9,)),
    ]
    return pl.pallas_call(
        functools.partial(kernel, n_seq, n_mp),
        out_shape=jax.ShapeDtypeStruct((ROWS, width), BF16),
        in_specs=[
            pl.BlockSpec(memory_space=pl.ANY if i in in_place else pltpu.VMEM)
            for i in range(len(args))
        ],
        out_specs=pl.BlockSpec(memory_space=pltpu.VMEM),
        scratch_shapes=scratch,
        compiler_params=pltpu.CompilerParams(
            collective_id=0, has_side_effects=True, vmem_limit_bytes=60 * 1024 * 1024
        ),
    )(*args)


def solution(mesh):
    seq, split, rows = P("seq", "mp"), P(None, "mp"), P("mp", None)
    vec, all_ = P("mp"), P()
    placed = (
        P("seq"), seq, seq, split, all_, all_, all_, split, split, split,
        all_, vec, split, all_, vec, split, vec, rows, split, rows,
    )
    return jax.shard_map(
        functools.partial(on_device, mesh.shape["seq"], mesh.shape["mp"]),
        mesh=mesh, in_specs=placed, out_specs=seq, check_vma=False,
    )
```

```python
import functools

import jax
import jax.numpy as jnp
from jax import lax
from jax.experimental import pallas as pl
from jax.experimental.pallas import tpu as pltpu
from jax.sharding import PartitionSpec as P

F32, BF16 = jnp.float32, jnp.bfloat16
HEAD = 64
ROWS = 128
PAIR = 128
LEVELS = 7
DECAY_SCALE = 0.606531
NORM_EPS = 1e-05
GROUP_EPS = 0.00064
UNIT_EPS = 1e-06
MESH = pl.DeviceIdType.MESH


def dot(a, b):
    return lax.dot_general(a, b, (((1,), (0,)), ((), ())), preferred_element_type=F32)


def dot_t(a, b):
    return lax.dot_general(a, b, (((1,), (1,)), ((), ())), preferred_element_type=F32)


def t_dot(a, b):
    return lax.dot_general(a, b, (((0,), (0,)), ((), ())), preferred_element_type=F32)


def halves(value):
    high = value.astype(BF16)
    return high, (value - high.astype(F32)).astype(BF16)


def iota2(shape, dim):
    return lax.broadcasted_iota(jnp.int32, shape, dim)


def left_half(shape):
    return iota2(shape, 1) % PAIR < HEAD


def layer_norm(values, gain):
    centered = values - jnp.mean(values, axis=-1, keepdims=True)
    spread = jnp.mean(centered * centered, axis=-1, keepdims=True)
    return centered * lax.rsqrt(spread + NORM_EPS) * gain


def masks_into(masks):
    row, col = iota2((ROWS, ROWS), 0), iota2((ROWS, ROWS), 1)
    for level in range(LEVELS):
        size = 1 << level
        same = row // (2 * size) == col // (2 * size)
        row_odd, col_odd = (row // size) % 2, (col // size) % 2
        masks[0, level] = jnp.where(same & (row_odd > col_odd), 1.0, 0.0).astype(BF16)
        masks[1, level] = jnp.where(same & (row_odd < col_odd), 1.0, 0.0).astype(BF16)


def two_heads(value):
    left = left_half(value.shape)
    zero = jnp.zeros_like(value)
    return jnp.concatenate([jnp.where(left, value, zero), jnp.where(left, zero, value)], axis=0)


def packed(value, head):
    half = value.shape[0] // 2
    upper, lower = value[:half], value[half:]
    left = left_half(upper.shape)
    if head == 0:
        return jnp.where(left, upper, pltpu.roll(lower, HEAD, 1))
    return jnp.where(left, pltpu.roll(upper, HEAD, 1), lower)


def unpacked(value):
    return jnp.concatenate([value, pltpu.roll(value, HEAD, 1)], axis=0)


def strand_rows(b, x_tile, idm, embf, st):
    for tile in range(8):
        slot, lanes = tile // 2, pl.ds((tile % 2) * PAIR, PAIR)
        added = embf[slot, 3:4, lanes]
        for letter in range(3):
            added = jnp.where(idm == float(letter), embf[slot, letter : letter + 1, lanes], added)
        st[b, :, tile * PAIR : (tile + 1) * PAIR] = (x_tile(tile) + added).astype(BF16)


def edge_row(piece, index, letter_of, embf, gain, keep):
    row = jnp.concatenate([piece[s].astype(F32)[index : index + 1] for s in range(4)], axis=1)
    letter = jnp.broadcast_to(letter_of, row.shape)
    emb = [jnp.concatenate([embf[s, c : c + 1] for s in range(4)], axis=1) for c in range(4)]
    added = emb[3]
    for c in range(3):
        added = jnp.where(letter == float(c), emb[c], added)
    row = (row + added).astype(BF16).astype(F32)
    return layer_norm(row, gain) * keep


def normed_and_mixed(b, st, nrm, mx, gain, mix):
    for chunk in range(4):
        rows = pl.ds(chunk * 32, 32)
        nrm[8 + chunk * 32 : 40 + chunk * 32] = layer_norm(st[b, rows].astype(F32), gain)
    for chunk in range(8):
        at = chunk * 16
        center = nrm[8 + at : 24 + at]
        before = nrm[7 + at : 23 + at] - center
        after = nrm[9 + at : 25 + at] - center
        for index in range(5):
            weight = mix[index : index + 1, :]
            mx[index, at : at + 16] = (center + before * weight).astype(BF16)
            mx[index, ROWS + at : ROWS + at + 16] = (center + after * weight).astype(BF16)


def projected(mx, wr, wk, wv, dfw, dbase, dsw, cfw, ibase, csw, proj):
    def keep(index, value):
        for beta in range(2):
            for q in range(2):
                proj[index, beta, q] = value[
                    beta * ROWS : (beta + 1) * ROWS, q * PAIR : (q + 1) * PAIR
                ]

    keep(0, dot(mx[0], wr[...]))
    key = dot(mx[1], wk[...])
    keep(1, key)
    keep(2, dot(mx[2], wv[...]))
    width = 2 * PAIR
    same_head = iota2((width, width), 0) // HEAD == iota2((width, width), 1) // HEAD
    ones = jnp.where(same_head, 1.0, 0.0).astype(BF16)
    high, low = halves(key * key)
    square = dot(high, ones) + dot(low, ones)
    keep(3, key * lax.rsqrt(square + UNIT_EPS))
    low_iclr = dot_t(mx[4], cfw[...]).astype(BF16)
    keep(4, jax.nn.sigmoid(ibase[...] + dot(low_iclr, csw[...])))
    low_decay = jnp.tanh(dot_t(mx[3], dfw[...])).astype(BF16)
    log_decay = -DECAY_SCALE * jax.nn.sigmoid(dbase[...] + dot(low_decay, dsw[...]))
    keep(5, log_decay)
    row, col = iota2((ROWS, ROWS), 0), iota2((ROWS, ROWS), 1)
    totals = []
    for beta in range(2):
        passed = (row >= col) if beta == 0 else (row <= col)
        ones = jnp.where(passed, 1.0, 0.0).astype(BF16)
        high, low = halves(log_decay[beta * ROWS : (beta + 1) * ROWS])
        totals.append(dot(ones, high) + dot(ones, low))
    keep(6, jnp.concatenate(totals, axis=0))


def block_terms(b, proj, masks, msg, aik, uw, vv, srd):
    row, col = iota2((ROWS, ROWS), 0), iota2((ROWS, ROWS), 1)
    eye = jnp.where(row == col, 1.0, 0.0).astype(BF16)
    chains, later = [], []
    for beta in range(2):
        strict = (row > col) if beta == 0 else (row < col)
        inclusive = (row >= col) if beta == 0 else (row <= col)
        for q in range(2):
            pair = (beta * 2 + b) * 2 + q
            receptance, key, value, unit, iclr, log_decay, total = [
                proj[i, beta, q] for i in range(7)
            ]
            middle = total[64:65] if beta == 0 else total[63:64]
            final = total[127:128] if beta == 0 else total[0:1]
            scale_right = jnp.exp(middle - total)
            left_prev = -unit * jnp.exp(total - log_decay - middle)
            left_here = receptance * jnp.exp(total - middle)
            right_insert = iclr * unit * scale_right
            right_key = key * scale_right
            from_start = jnp.exp(middle)
            to_end = jnp.exp(final - middle)
            left = jnp.concatenate(
                [two_heads(left_prev.astype(BF16)), two_heads(left_here.astype(BF16))], axis=0
            )
            right = jnp.concatenate([right_insert, right_key], axis=0).astype(BF16)
            scores = dot_t(left, right)
            pulls = []
            for head in range(2):
                at = head * ROWS
                lower = jnp.where(strict, scores[at : at + ROWS, :ROWS], 0.0).astype(BF16)
                chains.append([beta, lower, eye + lower * masks[beta, 0]])
                pulls.append(jnp.where(strict, scores[at : at + ROWS, ROWS:], 0.0).astype(BF16))
                read = 2 * ROWS + at
                aik[pair, :, at : at + ROWS] = jnp.where(
                    inclusive, scores[read : read + ROWS, :ROWS], 0.0
                ).astype(BF16)
                aik[pair, :, 2 * ROWS + at : 3 * ROWS + at] = jnp.where(
                    inclusive, scores[read : read + ROWS, ROWS:], 0.0
                ).astype(BF16)
            value = value.astype(BF16)
            vv[pair] = value
            srd[pair] = left_here * from_start
            pulled = dot(jnp.concatenate(pulls, axis=1), two_heads(value))
            wanted = jnp.concatenate([pulled, left_prev * from_start], axis=1).astype(BF16)
            tail_insert = (right_insert * to_end).astype(BF16)
            tail_key = (right_key * to_end).astype(BF16)
            later.append((pair, wanted, value, tail_insert, tail_key, final))
    for level in range(1, LEVELS):
        steps = [
            dot(inverse, lower * masks[beta, level]).astype(BF16)
            for beta, lower, inverse in chains
        ]
        for chain, step in zip(chains, steps):
            chain[2] = chain[2] + dot(step, chain[2]).astype(BF16)
    left_lanes = left_half((HEAD, PAIR))
    for index, (pair, wanted, value, tail_insert, tail_key, final) in enumerate(later):
        inverses = jnp.concatenate([chains[2 * index][2], chains[2 * index + 1][2]], axis=1)
        solved = dot(inverses, two_heads(wanted)).astype(BF16)
        uw[pair] = solved
        both = t_dot(solved, tail_insert)
        ends = both[:PAIR] + t_dot(value, tail_key)
        moved = both[PAIR:] + jnp.where(row == col, jnp.exp(final) - 1.0, 0.0)
        moved = jnp.where(left_lanes, moved[:HEAD], moved[HEAD:])
        ends = jnp.where(left_lanes, ends[:HEAD], ends[HEAD:])
        for head in range(2):
            moved_part = packed(moved, head).astype(BF16)
            for half in range(2):
                unit_at = pair * 4 + head * 2 + half
                msg[unit_at, 0:32] = moved_part
                msg[unit_at, 32:48] = packed(ends[half * 32 : half * 32 + 32], head).astype(BF16)


def local_terms(pair, aik, uw, vv, srd, local, start_map):
    solved = two_heads(uw[pair])
    scores = aik[pair]
    read = dot(scores[:, : 2 * ROWS], solved)
    keyed = dot(scores[:, 2 * ROWS :], two_heads(vv[pair]))
    local[pair] = read[:, :PAIR] + keyed
    start_map[pair] = (srd[pair] + read[:, PAIR:]).astype(BF16)


def scanned(n_seq, backward, recv, ret, inside, give):
    def place(i):
        return i + backward * (n_seq - 1 - 2 * i)

    size = 4
    groups = n_seq // size
    left = left_half((HEAD + 32, PAIR))
    blank = jnp.zeros((HEAD, PAIR), BF16)

    def block(i):
        value = recv[place(i)].astype(F32)
        whole = jnp.concatenate([unpacked(value[:32]), unpacked(value[32:])], axis=0)
        return jnp.where(left, whole, 0.0)

    def through(state, mapping):
        full = jnp.concatenate([mapping.astype(BF16), blank], axis=0)
        return dot(state.astype(BF16), full)

    for k in range(size):
        for g in range(groups):
            new = block(g * size + k)
            if k:
                so_far = inside[g * size + k - 1]
                new = so_far + new + through(so_far, new[:HEAD])
            inside[g * size + k] = new

    def onward(g, state):
        whole = inside[g * size + size - 1]
        for k in range(size):
            here = state
            if k:
                before = inside[g * size + k - 1]
                here = here + before[HEAD:] + through(here, before[:HEAD])
            ret[place(g * size + k)] = packed(here, 0).astype(BF16)

        return state + whole[HEAD:] + through(state, whole[:HEAD])

    lax.fori_loop(0, groups, onward, jnp.zeros((32, PAIR), F32))


def incoming(pair, states):
    rows = []
    left = left_half((16, PAIR))
    for head in range(2):
        for half in range(2):
            value = states[pair * 4 + head * 2 + half].astype(F32)
            turned = pltpu.roll(value, HEAD, 1)
            if head == 0:
                rows += [jnp.where(left, value, 0.0), jnp.where(left, turned, 0.0)]
            else:
                rows += [jnp.where(left, 0.0, turned), jnp.where(left, 0.0, value)]
    return jnp.concatenate(rows, axis=0).astype(BF16)


def grouped(pair, states, local, start_map, ones):
    out = local[pair] + dot_t(start_map[pair], incoming(pair, states))
    high, low = halves(out)
    centered = out - (dot(high, ones) + dot(low, ones)) * (1.0 / HEAD)
    spread = dot((centered * centered).astype(BF16), ones) * (1.0 / HEAD)
    return centered * lax.rsqrt(spread + GROUP_EPS)


def kernel(
    n_seq, n_mp,
    ids, hidden_fwd, hidden_rc, embed, gain1, gain2, mix,
    w_r, w_k, w_v, d_first, d_base, d_second, c_first, i_base, c_second,
    group_gain, w_out, ffn_key, ffn_value,
    out,
    wr, wk, wv, fk, fv, wo,
    xf, xr, rc_own, embf, prev, nxt, ids_prev, ids_next,
    st, nrm, mx, proj, masks, msg, recv, ret, states, aik, uw, vv, srd, local, start_map,
    joined, residual, act, part, got, inside,
    lsem, ss1, rs1, ss2, rs2, ss3, rs3, ss4, rs4,
):
    j, m = lax.axis_index("seq"), lax.axis_index("mp")

    def seq_at(offset):
        return lax.rem(j + offset + n_seq, n_seq)

    def mp_at(offset):
        return lax.rem(m + offset, n_mp)

    def send(src, dst, sems, index, device):
        copy = pltpu.make_async_remote_copy(
            src_ref=src, dst_ref=dst, send_sem=sems[0].at[index], recv_sem=sems[1].at[index],
            device_id=device, device_id_type=MESH,
        )
        copy.start()
        return copy

    def fetch(src, dst, index):
        copy = pltpu.make_async_copy(src, dst, lsem.at[index])
        copy.start()
        return copy

    barrier = pltpu.get_barrier_semaphore()

    def greet(seq_to, mp_to):
        pl.semaphore_signal(barrier, inc=1, device_id=(seq_to, mp_to), device_id_type=MESH)

    for k in range(1, n_mp):
        greet(j, mp_at(k))
        greet(seq_at(1), mp_at(k))
        greet(seq_at(-1), mp_at(k))

    def greet_far(d, carry):
        greet(seq_at(d), m)
        return carry

    lax.fori_loop(1, n_seq, greet_far, None)

    weights = [
        fetch(src, dst, i)
        for i, (src, dst) in enumerate(
            [(w_r, wr), (w_k, wk), (w_v, wv), (ffn_key, fk), (ffn_value, fv)]
        )
    ]
    own = [
        fetch(hidden_fwd, xf.at[m], 5),
        fetch(embed, embf.at[m], 6),
        fetch(w_out, wo.at[m], 7),
    ]
    masks_into(masks)
    pl.semaphore_wait(barrier, 3 * (n_mp - 1) + n_seq - 1)

    one = (ss1, rs1)
    copies = {}
    copies["mirror"] = send(hidden_rc, rc_own, one, 16, (n_seq - 1 - j, m))
    for k in range(1, n_mp):
        copies["emb", k] = send(embed, embf.at[m], one, 2 + k, (j, mp_at(k)))
        copies["fwd", k] = send(hidden_fwd, xf.at[m], one, k - 1, (j, mp_at(k)))
    for k in range(n_mp):
        copies["f_up", k] = send(
            hidden_fwd.at[pl.ds(ROWS - 16, 16)], prev.at[0, m], one, 6 + k, (seq_at(1), mp_at(k))
        )
        copies["f_down", k] = send(
            hidden_fwd.at[pl.ds(0, 16)], nxt.at[0, m], one, 10 + k, (seq_at(-1), mp_at(k))
        )
    copies["i_up"] = send(ids, ids_prev, one, 14, (seq_at(1), m))
    copies["i_down"] = send(ids, ids_next, one, 15, (seq_at(-1), m))

    letters = jnp.transpose(jnp.broadcast_to(ids[...].astype(F32), (ROWS, ROWS)))
    gain = gain1[...]
    has_prev = (j > 0).astype(F32)
    has_next = (j < n_seq - 1).astype(F32)

    def edges(b):
        sign, base = (1.0, 0.0) if b == 0 else (-1.0, 3.0)
        before = base + sign * ids_prev[0:1, ROWS - 1 : ROWS].astype(F32)
        after = base + sign * ids_next[0:1, 0:1].astype(F32)
        last, first = (15, 0) if b == 0 else (0, 15)
        nrm[7:8] = edge_row(prev.at[b], last, before, embf, gain, has_prev)
        nrm[136:137] = edge_row(nxt.at[b], first, after, embf, gain, has_next)

    def strand(b):
        normed_and_mixed(b, st, nrm, mx, gain, mix)
        projected(mx, wr, wk, wv, d_first, d_base, d_second, c_first, i_base, c_second, proj)
        block_terms(b, proj, masks, msg, aik, uw, vv, srd)

    def to_unit(d):
        return pltpu.make_async_remote_copy(
            src_ref=msg.at[seq_at(d)], dst_ref=recv.at[j],
            send_sem=ss2.at[d], recv_sem=rs2.at[d],
            device_id=(seq_at(d), m), device_id_type=MESH,
        )

    def give(block):
        @pl.when(block != j)
        def _():
            to_block(lax.rem(block - j + n_seq, n_seq)).start()

    def to_block(d):
        return pltpu.make_async_remote_copy(
            src_ref=ret.at[seq_at(d)], dst_ref=states.at[j],
            send_sem=ss3.at[d], recv_sem=rs3.at[d],
            device_id=(seq_at(d), m), device_id_type=MESH,
        )

    def each(action):
        def body(d, carry):
            action(d)
            return carry

        lax.fori_loop(1, n_seq, body, None)

    def give_units(b):
        def start(d):
            @pl.when(lax.rem(seq_at(d) // 8, 2) == b)
            def _():
                to_unit(d).start()

        each(start)

    copies["mirror"].wait_recv()
    for k in range(1, n_mp):
        copies["rc", k] = send(rc_own, xr.at[m], one, 16 + k, (j, mp_at(k)))
    for k in range(n_mp):
        copies["r_up", k] = send(
            rc_own.at[pl.ds(0, 16)], prev.at[1, m], one, 20 + k, (seq_at(1), mp_at(k))
        )
        copies["r_down", k] = send(
            rc_own.at[pl.ds(ROWS - 16, 16)], nxt.at[1, m], one, 24 + k, (seq_at(-1), mp_at(k))
        )
    own_rc = fetch(rc_own, xr.at[m], 8)
    sibling = m + 1 - 2 * lax.rem(m, 2)
    across = mp_at(2)
    copies["w_near"] = send(w_out, wo.at[m], one, 28, (j, sibling))
    copies["w_far"] = send(w_out, wo.at[m], one, 29, (j, across))

    for copy in own:
        copy.wait()
    for k in range(1, n_mp):
        copies["emb", k].wait_recv()
        copies["fwd", k].wait_recv()
    for k in range(n_mp):
        copies["f_up", k].wait_recv()
        copies["f_down", k].wait_recv()
    copies["i_up"].wait_recv()
    copies["i_down"].wait_recv()
    strand_rows(
        0, lambda t: xf[t // 2, :, (t % 2) * PAIR : (t % 2 + 1) * PAIR].astype(F32),
        letters, embf, st,
    )
    edges(0)
    for copy in weights[:3]:
        copy.wait()
    strand(0)
    give_units(0)

    own_rc.wait()
    for k in range(1, n_mp):
        copies["rc", k].wait_recv()
    for k in range(n_mp):
        copies["r_up", k].wait_recv()
        copies["r_down", k].wait_recv()
    turn = jnp.where(
        iota2((ROWS, ROWS), 0) + iota2((ROWS, ROWS), 1) == ROWS - 1, 1.0, 0.0
    ).astype(BF16)
    strand_rows(
        1, lambda t: dot(turn, xr[t // 2, :, (t % 2) * PAIR : (t % 2 + 1) * PAIR]),
        3.0 - letters, embf, st,
    )
    edges(1)
    strand(1)

    give_units(1)
    own_msg = fetch(msg.at[j], recv.at[j], 9)
    copies["w_far"].wait_recv()
    copies["w_on"] = send(wo.at[across], wo.at[across], one, 30, (j, sibling))

    def local_body(pair, carry):
        local_terms(pair, aik, uw, vv, srd, local, start_map)
        return carry

    lax.fori_loop(0, 8, local_body, None)
    own_msg.wait()
    each(lambda d: to_unit(d).wait_recv())
    scanned(n_seq, j // (n_seq // 2), recv, ret, inside, give)
    each(lambda d: to_block(d).start())
    own_ret = fetch(ret.at[j], states.at[j], 10)
    own_ret.wait()
    each(lambda d: to_block(d).wait_recv())

    same_head = iota2((PAIR, PAIR), 0) // HEAD == iota2((PAIR, PAIR), 1) // HEAD
    ones = jnp.where(same_head, 1.0, 0.0).astype(BF16)
    four = (ss4, rs4)
    for b in range(2):
        for q in range(2):
            total = grouped(b * 2 + q, states, local, start_map, ones) + grouped(
                4 + b * 2 + q, states, local, start_map, ones
            )
            lanes = slice(q * PAIR, (q + 1) * PAIR)
            joined[m, b * ROWS : (b + 1) * ROWS, lanes] = (
                total * group_gain[:, lanes]
            ).astype(BF16)
        block = joined.at[m, pl.ds(b * ROWS, ROWS)]
        copies["join", b, 1] = send(block, block, four, b * 3 + 1, (j, across))
        copies["join", b, 0] = send(block, block, four, b * 3, (j, sibling))
    for b in range(2):
        block = joined.at[across, pl.ds(b * ROWS, ROWS)]
        copies["join", b, 1].wait_recv()
        copies["join", b, 2] = send(block, block, four, b * 3 + 2, (j, sibling))

    copies["w_near"].wait_recv()
    copies["w_on"].wait_recv()
    for copy in weights[3:]:
        copy.wait()
    for b in range(2):
        copies["join", b, 0].wait_recv()
        copies["join", b, 2].wait_recv()
        rows = slice(b * ROWS, (b + 1) * ROWS)
        whole = st[b].astype(F32)
        for s in range(n_mp):
            whole = whole + dot(joined[s, rows], wo[s])
        residual[rows] = whole
        ffn_in = layer_norm(whole, gain2[...]).astype(BF16)
        act[rows] = jnp.square(jnp.maximum(dot(ffn_in, fk[...]), 0.0)).astype(BF16)

    def partial(index):
        lanes = pl.ds(pl.multiple_of(index * 2 * PAIR, PAIR), 2 * PAIR)
        both = dot(act[...], fv[:, lanes])
        return both[:ROWS] + both[ROWS:], lanes

    for k in range(1, n_mp):
        peer = mp_at(k)
        value, _ = partial(peer)
        part[k - 1] = value.astype(BF16)
        copies["sum", k] = send(part.at[k - 1], got.at[k - 1], four, 5 + k, (j, peer))
    value, lanes = partial(m)
    value = value + residual[:ROWS, lanes] + residual[ROWS:, lanes]
    for k in range(1, n_mp):
        copies["sum", k].wait_recv()
        value = value + got[k - 1].astype(F32)
    out[...] = value.astype(BF16)

    for copy in copies.values():
        copy.wait_send()
    each(lambda d: to_unit(d).wait_send())
    each(lambda d: to_block(d).wait_send())


def on_device(n_seq, n_mp, *args):
    args = list(args)
    args[0] = args[0].reshape(1, ROWS)
    for index in (4, 5, 11, 14, 16):
        args[index] = args[index].reshape(1, -1)
    for index in (10, 13):
        args[index] = args[index].T
    in_place = {1, 2, 7, 8, 9, 17, 18, 19}
    vmem = pltpu.VMEM
    dma = pltpu.SemaphoreType.DMA
    width = 2 * PAIR
    scratch = [
        vmem((1024, width), BF16), vmem((1024, width), BF16), vmem((1024, width), BF16),
        vmem((1024, 1024), BF16), vmem((1024, 1024), BF16), vmem((n_mp, width, 1024), BF16),
        vmem((n_mp, ROWS, width), BF16), vmem((n_mp, ROWS, width), BF16),
        vmem((ROWS, width), BF16), vmem((n_mp, 4, width), F32),
        vmem((2, n_mp, 16, width), BF16), vmem((2, n_mp, 16, width), BF16),
        vmem((1, ROWS), jnp.int32), vmem((1, ROWS), jnp.int32),
        vmem((2, ROWS, 1024), BF16), vmem((144, 1024), F32), vmem((5, 2 * ROWS, 1024), BF16),
        vmem((7, 2, 2, ROWS, PAIR), F32), vmem((2, LEVELS, ROWS, ROWS), BF16),
        vmem((32, 48, PAIR), BF16), vmem((n_seq, 48, PAIR), BF16),
        vmem((n_seq, 16, PAIR), BF16), vmem((32, 16, PAIR), BF16),
        vmem((8, ROWS, 4 * ROWS), BF16), vmem((8, ROWS, width), BF16),
        vmem((8, ROWS, PAIR), BF16), vmem((8, ROWS, PAIR), F32),
        vmem((8, ROWS, PAIR), F32), vmem((8, ROWS, PAIR), BF16),
        vmem((n_mp, 2 * ROWS, width), BF16), vmem((2 * ROWS, 1024), F32),
        vmem((2 * ROWS, 1024), BF16), vmem((3, ROWS, width), BF16), vmem((3, ROWS, width), BF16),
        vmem((n_seq, 96, PAIR), F32),
        dma((11,)), dma((32,)), dma((32,)), dma((n_seq,)), dma((n_seq,)),
        dma((n_seq,)), dma((n_seq,)), dma((9,)), dma((9,)),
    ]
    return pl.pallas_call(
        functools.partial(kernel, n_seq, n_mp),
        out_shape=jax.ShapeDtypeStruct((ROWS, width), BF16),
        in_specs=[
            pl.BlockSpec(memory_space=pl.ANY if i in in_place else pltpu.VMEM)
            for i in range(len(args))
        ],
        out_specs=pl.BlockSpec(memory_space=pltpu.VMEM),
        scratch_shapes=scratch,
        compiler_params=pltpu.CompilerParams(
            collective_id=0, has_side_effects=True, vmem_limit_bytes=60 * 1024 * 1024
        ),
    )(*args)


def solution(mesh):
    seq, split, rows = P("seq", "mp"), P(None, "mp"), P("mp", None)
    vec, all_ = P("mp"), P()
    placed = (
        P("seq"), seq, seq, split, all_, all_, all_, split, split, split,
        all_, vec, split, all_, vec, split, vec, rows, split, rows,
    )
    return jax.shard_map(
        functools.partial(on_device, mesh.shape["seq"], mesh.shape["mp"]),
        mesh=mesh, in_specs=placed, out_specs=seq, check_vma=False,
    )
```

```python
import functools

import jax
import jax.numpy as jnp
from jax import lax
from jax.experimental import pallas as pl
from jax.experimental.pallas import tpu as pltpu
from jax.sharding import PartitionSpec as P

F32, BF16 = jnp.float32, jnp.bfloat16
HEAD = 64
ROWS = 128
PAIR = 128
LEVELS = 7
DECAY_SCALE = 0.606531
NORM_EPS = 1e-05
GROUP_EPS = 0.00064
UNIT_EPS = 1e-06
MESH = pl.DeviceIdType.MESH


def dot(a, b):
    return lax.dot_general(a, b, (((1,), (0,)), ((), ())), preferred_element_type=F32)


def dot_t(a, b):
    return lax.dot_general(a, b, (((1,), (1,)), ((), ())), preferred_element_type=F32)


def t_dot(a, b):
    return lax.dot_general(a, b, (((0,), (0,)), ((), ())), preferred_element_type=F32)


def halves(value):
    high = value.astype(BF16)
    return high, (value - high.astype(F32)).astype(BF16)


def iota2(shape, dim):
    return lax.broadcasted_iota(jnp.int32, shape, dim)


def left_half(shape):
    return iota2(shape, 1) % PAIR < HEAD


def layer_norm(values, gain):
    centered = values - jnp.mean(values, axis=-1, keepdims=True)
    spread = jnp.mean(centered * centered, axis=-1, keepdims=True)
    return centered * lax.rsqrt(spread + NORM_EPS) * gain


def masks_into(masks):
    row, col = iota2((ROWS, ROWS), 0), iota2((ROWS, ROWS), 1)
    for level in range(LEVELS):
        size = 1 << level
        same = row // (2 * size) == col // (2 * size)
        row_odd, col_odd = (row // size) % 2, (col // size) % 2
        masks[0, level] = jnp.where(same & (row_odd > col_odd), 1.0, 0.0).astype(BF16)
        masks[1, level] = jnp.where(same & (row_odd < col_odd), 1.0, 0.0).astype(BF16)


def two_heads(value):
    left = left_half(value.shape)
    zero = jnp.zeros_like(value)
    return jnp.concatenate([jnp.where(left, value, zero), jnp.where(left, zero, value)], axis=0)


def on_diagonal(first, second):
    zero = jnp.zeros_like(first)
    upper = jnp.concatenate([first, zero], axis=1)
    return jnp.concatenate([upper, jnp.concatenate([zero, second], axis=1)], axis=0)


def packed(value, head):
    half = value.shape[0] // 2
    upper, lower = value[:half], value[half:]
    left = left_half(upper.shape)
    if head == 0:
        return jnp.where(left, upper, pltpu.roll(lower, HEAD, 1))
    return jnp.where(left, pltpu.roll(upper, HEAD, 1), lower)


def unpacked(value):
    return jnp.concatenate([value, pltpu.roll(value, HEAD, 1)], axis=0)


def strand_rows(b, x_tile, idm, embf, st):
    for tile in range(8):
        slot, lanes = tile // 2, pl.ds((tile % 2) * PAIR, PAIR)
        added = embf[slot, 3:4, lanes]
        for letter in range(3):
            added = jnp.where(idm == float(letter), embf[slot, letter : letter + 1, lanes], added)
        st[b, :, tile * PAIR : (tile + 1) * PAIR] = (x_tile(tile) + added).astype(BF16)


def edge_row(piece, index, letter_of, embf, gain, keep):
    row = jnp.concatenate([piece[s].astype(F32)[index : index + 1] for s in range(4)], axis=1)
    letter = jnp.broadcast_to(letter_of, row.shape)
    emb = [jnp.concatenate([embf[s, c : c + 1] for s in range(4)], axis=1) for c in range(4)]
    added = emb[3]
    for c in range(3):
        added = jnp.where(letter == float(c), emb[c], added)
    row = (row + added).astype(BF16).astype(F32)
    return layer_norm(row, gain) * keep


def normed_and_mixed(b, st, nrm, mx, gain, mix):
    for chunk in range(4):
        rows = pl.ds(chunk * 32, 32)
        nrm[8 + chunk * 32 : 40 + chunk * 32] = layer_norm(st[b, rows].astype(F32), gain)
    for chunk in range(8):
        at = chunk * 16
        center = nrm[8 + at : 24 + at]
        before = nrm[7 + at : 23 + at] - center
        after = nrm[9 + at : 25 + at] - center
        for index in range(5):
            weight = mix[index : index + 1, :]
            mx[index, at : at + 16] = (center + before * weight).astype(BF16)
            mx[index, ROWS + at : ROWS + at + 16] = (center + after * weight).astype(BF16)


def projected(mx, wr, wk, wv, dfw, dbase, dsw, cfw, ibase, csw, proj):
    def keep(index, value):
        for beta in range(2):
            for q in range(2):
                proj[index, beta, q] = value[
                    beta * ROWS : (beta + 1) * ROWS, q * PAIR : (q + 1) * PAIR
                ]

    keep(0, dot(mx[0], wr[...]))
    key = dot(mx[1], wk[...])
    keep(1, key)
    keep(2, dot(mx[2], wv[...]))
    width = 2 * PAIR
    same_head = iota2((width, width), 0) // HEAD == iota2((width, width), 1) // HEAD
    ones = jnp.where(same_head, 1.0, 0.0).astype(BF16)
    high, low = halves(key * key)
    square = dot(high, ones) + dot(low, ones)
    keep(3, key * lax.rsqrt(square + UNIT_EPS))
    low_iclr = dot_t(mx[4], cfw[...]).astype(BF16)
    keep(4, jax.nn.sigmoid(ibase[...] + dot(low_iclr, csw[...])))
    low_decay = jnp.tanh(dot_t(mx[3], dfw[...])).astype(BF16)
    log_decay = -DECAY_SCALE * jax.nn.sigmoid(dbase[...] + dot(low_decay, dsw[...]))
    keep(5, log_decay)
    row, col = iota2((ROWS, ROWS), 0), iota2((ROWS, ROWS), 1)
    totals = []
    for beta in range(2):
        passed = (row >= col) if beta == 0 else (row <= col)
        ones = jnp.where(passed, 1.0, 0.0).astype(BF16)
        high, low = halves(log_decay[beta * ROWS : (beta + 1) * ROWS])
        totals.append(dot(ones, high) + dot(ones, low))
    keep(6, jnp.concatenate(totals, axis=0))


def block_terms(b, proj, masks, msg, aik, uw, vv, srd):
    row, col = iota2((ROWS, ROWS), 0), iota2((ROWS, ROWS), 1)
    eye = jnp.where(row == col, 1.0, 0.0).astype(BF16)
    chains, later = [], []
    for beta in range(2):
        strict = (row > col) if beta == 0 else (row < col)
        inclusive = (row >= col) if beta == 0 else (row <= col)
        for q in range(2):
            pair = (beta * 2 + b) * 2 + q
            receptance, key, value, unit, iclr, log_decay, total = [
                proj[i, beta, q] for i in range(7)
            ]
            middle = total[64:65] if beta == 0 else total[63:64]
            final = total[127:128] if beta == 0 else total[0:1]
            scale_right = jnp.exp(middle - total)
            left_prev = -unit * jnp.exp(total - log_decay - middle)
            left_here = receptance * jnp.exp(total - middle)
            right_insert = iclr * unit * scale_right
            right_key = key * scale_right
            from_start = jnp.exp(middle)
            to_end = jnp.exp(final - middle)
            left = jnp.concatenate(
                [two_heads(left_prev.astype(BF16)), two_heads(left_here.astype(BF16))], axis=0
            )
            right = jnp.concatenate([right_insert, right_key], axis=0).astype(BF16)
            scores = dot_t(left, right)
            pulls, lowers = [], []
            for head in range(2):
                at = head * ROWS
                lower = jnp.where(strict, scores[at : at + ROWS, :ROWS], 0.0).astype(BF16)
                lowers.append(lower)
                pulls.append(jnp.where(strict, scores[at : at + ROWS, ROWS:], 0.0).astype(BF16))
                read = 2 * ROWS + at
                aik[pair, :, at : at + ROWS] = jnp.where(
                    inclusive, scores[read : read + ROWS, :ROWS], 0.0
                ).astype(BF16)
                aik[pair, :, 2 * ROWS + at : 3 * ROWS + at] = jnp.where(
                    inclusive, scores[read : read + ROWS, ROWS:], 0.0
                ).astype(BF16)
            inverse = jnp.concatenate([eye + lower * masks[beta, 0] for lower in lowers], axis=1)
            chains.append([beta, lowers, inverse])
            value = value.astype(BF16)
            vv[pair] = value
            srd[pair] = left_here * from_start
            pulled = dot(jnp.concatenate(pulls, axis=1), two_heads(value))
            wanted = jnp.concatenate([pulled, left_prev * from_start], axis=1).astype(BF16)
            tail_insert = (right_insert * to_end).astype(BF16)
            tail_key = (right_key * to_end).astype(BF16)
            later.append((pair, wanted, value, tail_insert, tail_key, final))
    for level in range(1, LEVELS):
        size = 1 << level
        steps = []
        for beta, lowers, inverse in chains:
            if size >= 16:
                starts = range(0 if beta else size, ROWS, 2 * size)
                inverse = jnp.concatenate([inverse[at : at + size] for at in starts], axis=0)
            level_mask = masks[beta, level]
            below = on_diagonal(*[lower * level_mask for lower in lowers])
            steps.append(dot(inverse, below).astype(BF16))
        for chain, step in zip(chains, steps):
            beta, _, inverse = chain
            step = dot(step, on_diagonal(inverse[:, :ROWS], inverse[:, ROWS:])).astype(BF16)
            if size >= 16:
                blocks = [inverse[at : at + size] for at in range(0, ROWS, size)]
                for index in range(ROWS // (2 * size)):
                    changed = 2 * index + 1 - beta
                    blocks[changed] = blocks[changed] + step[index * size : (index + 1) * size]
                chain[2] = jnp.concatenate(blocks, axis=0)
            else:
                chain[2] = inverse + step
    left_lanes = left_half((HEAD, PAIR))
    for index, (pair, wanted, value, tail_insert, tail_key, final) in enumerate(later):
        solved = dot(chains[index][2], two_heads(wanted)).astype(BF16)
        uw[pair] = solved
        both = t_dot(solved, tail_insert)
        ends = both[:PAIR] + t_dot(value, tail_key)
        moved = both[PAIR:] + jnp.where(row == col, jnp.exp(final) - 1.0, 0.0)
        moved = jnp.where(left_lanes, moved[:HEAD], moved[HEAD:])
        ends = jnp.where(left_lanes, ends[:HEAD], ends[HEAD:])
        for head in range(2):
            moved_part = packed(moved, head).astype(BF16)
            for half in range(2):
                unit_at = pair * 4 + head * 2 + half
                msg[unit_at, 0:32] = moved_part
                msg[unit_at, 32:48] = packed(ends[half * 32 : half * 32 + 32], head).astype(BF16)


def local_terms(pair, aik, uw, vv, srd, local, start_map):
    solved = two_heads(uw[pair])
    scores = aik[pair]
    read = dot(scores[:, : 2 * ROWS], solved)
    keyed = dot(scores[:, 2 * ROWS :], two_heads(vv[pair]))
    local[pair] = read[:, :PAIR] + keyed
    start_map[pair] = (srd[pair] + read[:, PAIR:]).astype(BF16)


def scanned(n_seq, backward, recv, ret, inside, give):
    def place(i):
        return i + backward * (n_seq - 1 - 2 * i)

    size = 4
    groups = n_seq // size
    left = left_half((HEAD + 32, PAIR))
    blank = jnp.zeros((HEAD, PAIR), BF16)

    def block(i):
        value = recv[place(i)].astype(F32)
        whole = jnp.concatenate([unpacked(value[:32]), unpacked(value[32:])], axis=0)
        return jnp.where(left, whole, 0.0)

    def through(state, mapping):
        full = jnp.concatenate([mapping.astype(BF16), blank], axis=0)
        return dot(state.astype(BF16), full)

    for k in range(size):
        for g in range(groups):
            new = block(g * size + k)
            if k:
                so_far = inside[g * size + k - 1]
                new = so_far + new + through(so_far, new[:HEAD])
            inside[g * size + k] = new

    def onward(g, state):
        whole = inside[g * size + size - 1]
        for k in range(size):
            here = state
            if k:
                before = inside[g * size + k - 1]
                here = here + before[HEAD:] + through(here, before[:HEAD])
            ret[place(g * size + k)] = packed(here, 0).astype(BF16)

        return state + whole[HEAD:] + through(state, whole[:HEAD])

    lax.fori_loop(0, groups, onward, jnp.zeros((32, PAIR), F32))


def incoming(pair, states):
    rows = []
    left = left_half((16, PAIR))
    for head in range(2):
        for half in range(2):
            value = states[pair * 4 + head * 2 + half].astype(F32)
            turned = pltpu.roll(value, HEAD, 1)
            if head == 0:
                rows += [jnp.where(left, value, 0.0), jnp.where(left, turned, 0.0)]
            else:
                rows += [jnp.where(left, 0.0, turned), jnp.where(left, 0.0, value)]
    return jnp.concatenate(rows, axis=0).astype(BF16)


def grouped(pair, states, local, start_map, ones):
    out = local[pair] + dot_t(start_map[pair], incoming(pair, states))
    high, low = halves(out)
    centered = out - (dot(high, ones) + dot(low, ones)) * (1.0 / HEAD)
    spread = dot((centered * centered).astype(BF16), ones) * (1.0 / HEAD)
    return centered * lax.rsqrt(spread + GROUP_EPS)


def kernel(
    n_seq, n_mp,
    ids_in, hidden_fwd, hidden_rc, embed, gain1_in, gain2_in, mix_in,
    w_r, w_k, w_v, d_first_in, d_base_in, d_second_in, c_first_in, i_base_in, c_second_in,
    group_gain_in, w_out, ffn_key, ffn_value,
    out,
    ids, gain1, gain2, mix, d_first, d_base, d_second, c_first, i_base, c_second, group_gain,
    wr, wk, wv, fk, fv, wo,
    xf, xr, embf, prev, nxt, ids_prev, ids_next,
    st, nrm, mx, proj, masks, msg, recv, ret, states, aik, uw, vv, srd, local, start_map,
    joined, residual, act, part, got, inside,
    lsem, ss1, rs1, ss2, rs2, ss3, rs3, ss4, rs4,
):
    j, m = lax.axis_index("seq"), lax.axis_index("mp")

    def seq_at(offset):
        return lax.rem(j + offset + n_seq, n_seq)

    def mp_at(offset):
        return lax.rem(m + offset, n_mp)

    def send(src, dst, sems, index, device):
        copy = pltpu.make_async_remote_copy(
            src_ref=src, dst_ref=dst, send_sem=sems[0].at[index], recv_sem=sems[1].at[index],
            device_id=device, device_id_type=MESH,
        )
        copy.start()
        return copy

    def edge_act(act_remote, act_local):
        for up in (True, False):
            rows, place, seq_to = (0, prev, above) if up else (ROWS - 16, nxt, below)
            source, target = hidden_rc.at[pl.ds(rows, 16)], place.at[1, m]

            def remote(k, index=20 if up else 24, source=source, target=target, seq_to=seq_to):
                act_remote(
                    pltpu.make_async_remote_copy(
                        src_ref=source, dst_ref=target,
                        send_sem=ss1.at[index + k], recv_sem=rs1.at[index + k],
                        device_id=(seq_to, mp_at(k)), device_id_type=MESH,
                    )
                )

            pl.when(seq_to != j)(functools.partial(remote, 0))
            for k in range(1, n_mp):
                remote(k)
            if act_local is not None:

                @pl.when(seq_to == j)
                def _(source=source, target=target, sem=lsem.at[21 + int(up)]):
                    act_local(pltpu.make_async_copy(source, target, sem))

    def fetch(src, dst, index):
        copy = pltpu.make_async_copy(src, dst, lsem.at[index])
        copy.start()
        return copy

    barrier = pltpu.get_barrier_semaphore()

    above, below = lax.rem(n_seq - j, n_seq), lax.rem(2 * n_seq - 2 - j, n_seq)

    def greet(seq_to, mp_to):
        pl.semaphore_signal(barrier, inc=1, device_id=(seq_to, mp_to), device_id_type=MESH)

    for k in range(1, n_mp):
        greet(j, mp_at(k))
        greet(seq_at(1), mp_at(k))
        greet(seq_at(-1), mp_at(k))
        greet(above, mp_at(k))
        greet(below, mp_at(k))

    def greet_far(d, carry):
        greet(seq_at(d), m)
        return carry

    lax.fori_loop(1, n_seq, greet_far, None)
    greet(n_seq - 1 - j, mp_at(2))
    greet(j + 4 - 8 * lax.rem(j // 4, 2), mp_at(2))

    weights = [
        fetch(src, dst, i)
        for i, (src, dst) in enumerate(
            [(w_r, wr), (w_k, wk), (w_v, wv), (ffn_key, fk), (ffn_value, fv)]
        )
    ]
    own = [
        fetch(src, dst, 5 + i)
        for i, (src, dst) in enumerate(
            [
                (hidden_fwd, xf.at[m]), (embed, embf.at[m]), (ids_in, ids), (gain1_in, gain1),
                (mix_in, mix), (d_first_in, d_first), (d_base_in, d_base),
                (d_second_in, d_second), (c_first_in, c_first), (i_base_in, i_base),
                (c_second_in, c_second), (gain2_in, gain2), (group_gain_in, group_gain),
                (w_out, wo.at[m]),
            ]
        )
    ]
    masks_into(masks)
    pl.semaphore_wait(barrier, 5 * (n_mp - 1) + n_seq + 1)

    one = (ss1, rs1)
    copies = {}
    sibling = m + 1 - 2 * lax.rem(m, 2)
    across = mp_at(2)
    mirrored = n_seq - 1 - j
    flipped = j + 4 - 8 * lax.rem(j // 4, 2)
    copies["fwd", 1] = send(hidden_fwd, xf.at[m], one, 1, (j, across))
    copies["fwd", 0] = send(hidden_fwd, xf.at[m], one, 0, (j, sibling))
    for k in range(n_mp):
        copies["f_up", k] = send(
            hidden_fwd.at[pl.ds(ROWS - 16, 16)], prev.at[0, m], one, 6 + k, (seq_at(1), mp_at(k))
        )
        copies["f_down", k] = send(
            hidden_fwd.at[pl.ds(0, 16)], nxt.at[0, m], one, 10 + k, (seq_at(-1), mp_at(k))
        )
    copies["i_up"] = send(ids_in, ids_prev, one, 14, (seq_at(1), m))
    copies["i_down"] = send(ids_in, ids_next, one, 15, (seq_at(-1), m))
    for k in range(1, n_mp):
        copies["emb", k] = send(embed, embf.at[m], one, 2 + k, (j, mp_at(k)))
    edge_act(lambda copy: copy.start(), lambda copy: copy.start())
    copies["rc", 0] = send(hidden_rc, xr.at[m], one, 16, (mirrored, m))
    copies["rc", 1] = send(hidden_rc, xr.at[m], one, 17, (mirrored, across))

    has_prev = (j > 0).astype(F32)
    has_next = (j < n_seq - 1).astype(F32)

    def edges(b):
        sign, base = (1.0, 0.0) if b == 0 else (-1.0, 3.0)
        before = base + sign * ids_prev[0:1, ROWS - 1 : ROWS].astype(F32)
        after = base + sign * ids_next[0:1, 0:1].astype(F32)
        last, first = (15, 0) if b == 0 else (0, 15)
        gain = gain1[...]
        nrm[7:8] = edge_row(prev.at[b], last, before, embf, gain, has_prev)
        nrm[136:137] = edge_row(nxt.at[b], first, after, embf, gain, has_next)

    def strand(b):
        projected(mx, wr, wk, wv, d_first, d_base, d_second, c_first, i_base, c_second, proj)
        block_terms(b, proj, masks, msg, aik, uw, vv, srd)

    def to_unit(d):
        return pltpu.make_async_remote_copy(
            src_ref=msg.at[seq_at(d)], dst_ref=recv.at[j],
            send_sem=ss2.at[d], recv_sem=rs2.at[d],
            device_id=(seq_at(d), m), device_id_type=MESH,
        )

    def give(block):
        @pl.when(block != j)
        def _():
            to_block(lax.rem(block - j + n_seq, n_seq)).start()

    def to_block(d):
        return pltpu.make_async_remote_copy(
            src_ref=ret.at[seq_at(d)], dst_ref=states.at[j],
            send_sem=ss3.at[d], recv_sem=rs3.at[d],
            device_id=(seq_at(d), m), device_id_type=MESH,
        )

    def each(action):
        def body(d, carry):
            action(d)
            return carry

        lax.fori_loop(1, n_seq, body, None)

    def give_units(b):
        def start(d):
            @pl.when(lax.rem(seq_at(d) // 8, 2) == b)
            def _():
                to_unit(d).start()

        each(start)

    copies["fwd", 1].wait_recv()
    copies["fwd", 2] = send(xf.at[across], xf.at[across], one, 2, (j, sibling))
    for copy in own:
        copy.wait()
    letters = jnp.transpose(jnp.broadcast_to(ids[...].astype(F32), (ROWS, ROWS)))
    for k in range(1, n_mp):
        copies["emb", k].wait_recv()
    copies["fwd", 0].wait_recv()
    copies["fwd", 2].wait_recv()
    for k in range(n_mp):
        copies["f_up", k].wait_recv()
        copies["f_down", k].wait_recv()
    copies["i_up"].wait_recv()
    copies["i_down"].wait_recv()
    strand_rows(
        0, lambda t: xf[t // 2, :, (t % 2) * PAIR : (t % 2 + 1) * PAIR].astype(F32),
        letters, embf, st,
    )
    edges(0)
    normed_and_mixed(0, st, nrm, mx, gain1[...], mix)

    copies["rc", 0].wait_recv()
    copies["rc", 2] = send(xr.at[m], xr.at[m], one, 18, (j, sibling))
    copies["rc", 1].wait_recv()
    copies["rc", 3] = send(xr.at[across], xr.at[across], one, 19, (j, sibling))
    copies["w_near"] = send(w_out, wo.at[m], one, 28, (j, sibling))
    copies["w_far"] = send(w_out, wo.at[m], one, 29, (flipped, across))
    for copy in weights[:3]:
        copy.wait()
    strand(0)
    give_units(0)

    copies["rc", 2].wait_recv()
    copies["rc", 3].wait_recv()
    edge_act(lambda copy: copy.wait_recv(), lambda copy: copy.wait())
    turn = jnp.where(
        iota2((ROWS, ROWS), 0) + iota2((ROWS, ROWS), 1) == ROWS - 1, 1.0, 0.0
    ).astype(BF16)
    strand_rows(
        1, lambda t: dot(turn, xr[t // 2, :, (t % 2) * PAIR : (t % 2 + 1) * PAIR]),
        3.0 - letters, embf, st,
    )
    edges(1)
    normed_and_mixed(1, st, nrm, mx, gain1[...], mix)
    strand(1)

    give_units(1)
    own_msg = fetch(msg.at[j], recv.at[j], 19)
    copies["w_far"].wait_recv()
    copies["w_on"] = send(wo.at[across], wo.at[across], one, 30, (j, sibling))

    def local_body(pair, carry):
        local_terms(pair, aik, uw, vv, srd, local, start_map)
        return carry

    lax.fori_loop(0, 8, local_body, None)
    own_msg.wait()
    each(lambda d: to_unit(d).wait_recv())
    scanned(n_seq, j // (n_seq // 2), recv, ret, inside, give)
    each(lambda d: to_block(d).start())
    own_ret = fetch(ret.at[j], states.at[j], 20)
    own_ret.wait()
    each(lambda d: to_block(d).wait_recv())

    same_head = iota2((PAIR, PAIR), 0) // HEAD == iota2((PAIR, PAIR), 1) // HEAD
    ones = jnp.where(same_head, 1.0, 0.0).astype(BF16)
    four = (ss4, rs4)
    for b in range(2):
        for q in range(2):
            total = grouped(b * 2 + q, states, local, start_map, ones) + grouped(
                4 + b * 2 + q, states, local, start_map, ones
            )
            lanes = slice(q * PAIR, (q + 1) * PAIR)
            joined[m, b * ROWS : (b + 1) * ROWS, lanes] = (
                total * group_gain[:, lanes]
            ).astype(BF16)
        block = joined.at[m, pl.ds(b * ROWS, ROWS)]
        copies["join", b, 1] = send(block, block, four, b * 3 + 1, (j, across))
        copies["join", b, 0] = send(block, block, four, b * 3, (j, sibling))
    for b in range(2):
        block = joined.at[across, pl.ds(b * ROWS, ROWS)]
        copies["join", b, 1].wait_recv()
        copies["join", b, 2] = send(block, block, four, b * 3 + 2, (j, sibling))

    copies["w_near"].wait_recv()
    copies["w_on"].wait_recv()
    for copy in weights[3:]:
        copy.wait()
    for b in range(2):
        copies["join", b, 0].wait_recv()
        copies["join", b, 2].wait_recv()
        rows = slice(b * ROWS, (b + 1) * ROWS)
        whole = st[b].astype(F32)
        for s in range(n_mp):
            whole = whole + dot(joined[s, rows], wo[s])
        residual[rows] = whole
        ffn_in = layer_norm(whole, gain2[...]).astype(BF16)
        act[rows] = jnp.square(jnp.maximum(dot(ffn_in, fk[...]), 0.0)).astype(BF16)

    def partial(index):
        lanes = pl.ds(pl.multiple_of(index * 2 * PAIR, PAIR), 2 * PAIR)
        both = dot(act[...], fv[:, lanes])
        return both[:ROWS] + both[ROWS:], lanes

    for k, peer in enumerate((across, lax.rem(sibling + 2, n_mp), sibling)):
        value, _ = partial(peer)
        part[k] = value.astype(BF16)
        copies["sum", k] = send(part.at[k], got.at[k], four, 6 + k, (j, peer))
    value, lanes = partial(m)
    value = value + residual[:ROWS, lanes] + residual[ROWS:, lanes]
    for k in (2, 0, 1):
        copies["sum", k].wait_recv()
        value = value + got[k].astype(F32)
    out[...] = value.astype(BF16)

    for copy in copies.values():
        copy.wait_send()
    edge_act(lambda copy: copy.wait_send(), None)
    each(lambda d: to_unit(d).wait_send())
    each(lambda d: to_block(d).wait_send())


def on_device(n_seq, n_mp, *args):
    args = list(args)
    args[0] = args[0].reshape(1, ROWS)
    for index in (4, 5, 11, 14, 16):
        args[index] = args[index].reshape(1, -1)
    for index in (10, 13):
        args[index] = args[index].T
    vmem = pltpu.VMEM
    dma = pltpu.SemaphoreType.DMA
    width = 2 * PAIR
    scratch = [
        vmem((1, ROWS), jnp.int32), vmem((1, 1024), F32), vmem((1, 1024), F32),
        vmem((5, 1024), F32), vmem((64, 1024), BF16), vmem((1, width), F32),
        vmem((64, width), BF16), vmem((64, 1024), BF16), vmem((1, width), F32),
        vmem((64, width), BF16), vmem((1, width), F32),
        vmem((1024, width), BF16), vmem((1024, width), BF16), vmem((1024, width), BF16),
        vmem((1024, 1024), BF16), vmem((1024, 1024), BF16), vmem((n_mp, width, 1024), BF16),
        vmem((n_mp, ROWS, width), BF16), vmem((n_mp, ROWS, width), BF16),
        vmem((n_mp, 4, width), F32),
        vmem((2, n_mp, 16, width), BF16), vmem((2, n_mp, 16, width), BF16),
        vmem((1, ROWS), jnp.int32), vmem((1, ROWS), jnp.int32),
        vmem((2, ROWS, 1024), BF16), vmem((144, 1024), F32), vmem((5, 2 * ROWS, 1024), BF16),
        vmem((7, 2, 2, ROWS, PAIR), F32), vmem((2, LEVELS, ROWS, ROWS), BF16),
        vmem((32, 48, PAIR), BF16), vmem((n_seq, 48, PAIR), BF16),
        vmem((n_seq, 16, PAIR), BF16), vmem((32, 16, PAIR), BF16),
        vmem((8, ROWS, 4 * ROWS), BF16), vmem((8, ROWS, width), BF16),
        vmem((8, ROWS, PAIR), BF16), vmem((8, ROWS, PAIR), F32),
        vmem((8, ROWS, PAIR), F32), vmem((8, ROWS, PAIR), BF16),
        vmem((n_mp, 2 * ROWS, width), BF16), vmem((2 * ROWS, 1024), F32),
        vmem((2 * ROWS, 1024), BF16), vmem((3, ROWS, width), BF16), vmem((3, ROWS, width), BF16),
        vmem((n_seq, 96, PAIR), F32),
        dma((23,)), dma((32,)), dma((32,)), dma((n_seq,)), dma((n_seq,)),
        dma((n_seq,)), dma((n_seq,)), dma((9,)), dma((9,)),
    ]
    return pl.pallas_call(
        functools.partial(kernel, n_seq, n_mp),
        out_shape=jax.ShapeDtypeStruct((ROWS, width), BF16),
        in_specs=[
            pl.BlockSpec(memory_space=pl.ANY)
            for _ in args
        ],
        out_specs=pl.BlockSpec(memory_space=pltpu.VMEM),
        scratch_shapes=scratch,
        compiler_params=pltpu.CompilerParams(
            collective_id=0, has_side_effects=True, vmem_limit_bytes=60 * 1024 * 1024
        ),
    )(*args)


def solution(mesh):
    seq, split, rows = P("seq", "mp"), P(None, "mp"), P("mp", None)
    vec, all_ = P("mp"), P()
    placed = (
        P("seq"), seq, seq, split, all_, all_, all_, split, split, split,
        all_, vec, split, all_, vec, split, vec, rows, split, rows,
    )
    return jax.shard_map(
        functools.partial(on_device, mesh.shape["seq"], mesh.shape["mp"]),
        mesh=mesh, in_specs=placed, out_specs=seq, check_vma=False,
    )
```

```python
import functools

import jax
import jax.numpy as jnp
from jax import lax
from jax.experimental import pallas as pl
from jax.experimental.pallas import tpu as pltpu
from jax.sharding import PartitionSpec as P

F32, BF16 = jnp.float32, jnp.bfloat16
HEAD = 64
ROWS = 128
PAIR = 128
LEVELS = 7
DECAY_SCALE = 0.606531
NORM_EPS = 1e-05
GROUP_EPS = 0.00064
UNIT_EPS = 1e-06
MESH = pl.DeviceIdType.MESH


def dot(a, b):
    return lax.dot_general(a, b, (((1,), (0,)), ((), ())), preferred_element_type=F32)


def dot_t(a, b):
    return lax.dot_general(a, b, (((1,), (1,)), ((), ())), preferred_element_type=F32)


def t_dot(a, b):
    return lax.dot_general(a, b, (((0,), (0,)), ((), ())), preferred_element_type=F32)


def halves(value):
    high = value.astype(BF16)
    return high, (value - high.astype(F32)).astype(BF16)


def iota2(shape, dim):
    return lax.broadcasted_iota(jnp.int32, shape, dim)


def left_half(shape):
    return iota2(shape, 1) % PAIR < HEAD


def layer_norm(values, gain):
    centered = values - jnp.mean(values, axis=-1, keepdims=True)
    spread = jnp.mean(centered * centered, axis=-1, keepdims=True)
    return centered * lax.rsqrt(spread + NORM_EPS) * gain


def masks_into(masks):
    row, col = iota2((ROWS, ROWS), 0), iota2((ROWS, ROWS), 1)
    for level in range(LEVELS):
        size = 1 << level
        same = row // (2 * size) == col // (2 * size)
        row_odd, col_odd = (row // size) % 2, (col // size) % 2
        masks[0, level] = jnp.where(same & (row_odd > col_odd), 1.0, 0.0).astype(BF16)
        masks[1, level] = jnp.where(same & (row_odd < col_odd), 1.0, 0.0).astype(BF16)


def two_heads(value):
    left = left_half(value.shape)
    zero = jnp.zeros_like(value)
    return jnp.concatenate([jnp.where(left, value, zero), jnp.where(left, zero, value)], axis=0)


def on_diagonal(first, second):
    zero = jnp.zeros_like(first)
    upper = jnp.concatenate([first, zero], axis=1)
    return jnp.concatenate([upper, jnp.concatenate([zero, second], axis=1)], axis=0)


def packed(value, head):
    half = value.shape[0] // 2
    upper, lower = value[:half], value[half:]
    left = left_half(upper.shape)
    if head == 0:
        return jnp.where(left, upper, pltpu.roll(lower, HEAD, 1))
    return jnp.where(left, pltpu.roll(upper, HEAD, 1), lower)


def unpacked(value):
    return jnp.concatenate([value, pltpu.roll(value, HEAD, 1)], axis=0)


def strand_rows(b, x_tile, idm, embf, st):
    for tile in range(8):
        slot, lanes = tile // 2, pl.ds((tile % 2) * PAIR, PAIR)
        added = embf[slot, 3:4, lanes]
        for letter in range(3):
            added = jnp.where(idm == float(letter), embf[slot, letter : letter + 1, lanes], added)
        st[b, :, tile * PAIR : (tile + 1) * PAIR] = (x_tile(tile) + added).astype(BF16)


def edge_row(piece, index, letter_of, embf, gain, keep):
    row = jnp.concatenate([piece[s].astype(F32)[index : index + 1] for s in range(4)], axis=1)
    letter = jnp.broadcast_to(letter_of, row.shape)
    emb = [jnp.concatenate([embf[s, c : c + 1] for s in range(4)], axis=1) for c in range(4)]
    added = emb[3]
    for c in range(3):
        added = jnp.where(letter == float(c), emb[c], added)
    row = (row + added).astype(BF16).astype(F32)
    return layer_norm(row, gain) * keep


def normed_and_mixed(b, st, nrm, mx, gain, mix):
    for chunk in range(4):
        rows = pl.ds(chunk * 32, 32)
        nrm[8 + chunk * 32 : 40 + chunk * 32] = layer_norm(st[b, rows].astype(F32), gain)
    for chunk in range(8):
        at = chunk * 16
        center = nrm[8 + at : 24 + at]
        before = nrm[7 + at : 23 + at] - center
        after = nrm[9 + at : 25 + at] - center
        for index in range(5):
            weight = mix[index : index + 1, :]
            mx[index, at : at + 16] = (center + before * weight).astype(BF16)
            mx[index, ROWS + at : ROWS + at + 16] = (center + after * weight).astype(BF16)


def projected(mx, wr, wk, wv, dfw, dbase, dsw, cfw, ibase, csw, proj):
    def keep(index, value):
        for beta in range(2):
            for q in range(2):
                proj[index, beta, q] = value[
                    beta * ROWS : (beta + 1) * ROWS, q * PAIR : (q + 1) * PAIR
                ]

    keep(0, dot(mx[0], wr[...]))
    key = dot(mx[1], wk[...])
    keep(1, key)
    keep(2, dot(mx[2], wv[...]))
    width = 2 * PAIR
    same_head = iota2((width, width), 0) // HEAD == iota2((width, width), 1) // HEAD
    ones = jnp.where(same_head, 1.0, 0.0).astype(BF16)
    high, low = halves(key * key)
    square = dot(high, ones) + dot(low, ones)
    keep(3, key * lax.rsqrt(square + UNIT_EPS))
    low_iclr = dot_t(mx[4], cfw[...]).astype(BF16)
    keep(4, jax.nn.sigmoid(ibase[...] + dot(low_iclr, csw[...])))
    low_decay = jnp.tanh(dot_t(mx[3], dfw[...])).astype(BF16)
    log_decay = -DECAY_SCALE * jax.nn.sigmoid(dbase[...] + dot(low_decay, dsw[...]))
    keep(5, log_decay)
    row, col = iota2((ROWS, ROWS), 0), iota2((ROWS, ROWS), 1)
    totals = []
    for beta in range(2):
        passed = (row >= col) if beta == 0 else (row <= col)
        ones = jnp.where(passed, 1.0, 0.0).astype(BF16)
        high, low = halves(log_decay[beta * ROWS : (beta + 1) * ROWS])
        totals.append(dot(ones, high) + dot(ones, low))
    keep(6, jnp.concatenate(totals, axis=0))


def block_terms(b, proj, masks, msg, aik, uw, vv, srd):
    row, col = iota2((ROWS, ROWS), 0), iota2((ROWS, ROWS), 1)
    eye = jnp.where(row == col, 1.0, 0.0).astype(BF16)
    chains, later = [], []
    for beta in range(2):
        strict = (row > col) if beta == 0 else (row < col)
        inclusive = (row >= col) if beta == 0 else (row <= col)
        for q in range(2):
            pair = (beta * 2 + b) * 2 + q
            receptance, key, value, unit, iclr, log_decay, total = [
                proj[i, beta, q] for i in range(7)
            ]
            middle = total[64:65] if beta == 0 else total[63:64]
            final = total[127:128] if beta == 0 else total[0:1]
            scale_right = jnp.exp(middle - total)
            left_prev = -unit * jnp.exp(total - log_decay - middle)
            left_here = receptance * jnp.exp(total - middle)
            right_insert = iclr * unit * scale_right
            right_key = key * scale_right
            from_start = jnp.exp(middle)
            to_end = jnp.exp(final - middle)
            left = jnp.concatenate(
                [two_heads(left_prev.astype(BF16)), two_heads(left_here.astype(BF16))], axis=0
            )
            right = jnp.concatenate([right_insert, right_key], axis=0).astype(BF16)
            scores = dot_t(left, right)
            pulls, lowers = [], []
            for head in range(2):
                at = head * ROWS
                lower = jnp.where(strict, scores[at : at + ROWS, :ROWS], 0.0).astype(BF16)
                lowers.append(lower)
                pulls.append(jnp.where(strict, scores[at : at + ROWS, ROWS:], 0.0).astype(BF16))
                read = 2 * ROWS + at
                aik[pair, :, at : at + ROWS] = jnp.where(
                    inclusive, scores[read : read + ROWS, :ROWS], 0.0
                ).astype(BF16)
                aik[pair, :, 2 * ROWS + at : 3 * ROWS + at] = jnp.where(
                    inclusive, scores[read : read + ROWS, ROWS:], 0.0
                ).astype(BF16)
            inverse = jnp.concatenate([eye + lower * masks[beta, 0] for lower in lowers], axis=1)
            chains.append([beta, lowers, inverse])
            value = value.astype(BF16)
            vv[pair] = value
            srd[pair] = left_here * from_start
            pulled = dot(jnp.concatenate(pulls, axis=1), two_heads(value))
            wanted = jnp.concatenate([pulled, left_prev * from_start], axis=1).astype(BF16)
            tail_insert = (right_insert * to_end).astype(BF16)
            tail_key = (right_key * to_end).astype(BF16)
            later.append((pair, wanted, value, tail_insert, tail_key, final))
    for level in range(1, LEVELS):
        size = 1 << level
        steps = []
        for beta, lowers, inverse in chains:
            if size >= 16:
                starts = range(0 if beta else size, ROWS, 2 * size)
                inverse = jnp.concatenate([inverse[at : at + size] for at in starts], axis=0)
            level_mask = masks[beta, level]
            below = on_diagonal(*[lower * level_mask for lower in lowers])
            steps.append(dot(inverse, below).astype(BF16))
        for chain, step in zip(chains, steps):
            beta, _, inverse = chain
            step = dot(step, on_diagonal(inverse[:, :ROWS], inverse[:, ROWS:])).astype(BF16)
            if size >= 16:
                blocks = [inverse[at : at + size] for at in range(0, ROWS, size)]
                for index in range(ROWS // (2 * size)):
                    changed = 2 * index + 1 - beta
                    blocks[changed] = blocks[changed] + step[index * size : (index + 1) * size]
                chain[2] = jnp.concatenate(blocks, axis=0)
            else:
                chain[2] = inverse + step
    left_lanes = left_half((HEAD, PAIR))
    for index, (pair, wanted, value, tail_insert, tail_key, final) in enumerate(later):
        solved = dot(chains[index][2], two_heads(wanted)).astype(BF16)
        uw[pair] = solved
        both = t_dot(solved, tail_insert)
        ends = both[:PAIR] + t_dot(value, tail_key)
        moved = both[PAIR:] + jnp.where(row == col, jnp.exp(final) - 1.0, 0.0)
        moved = jnp.where(left_lanes, moved[:HEAD], moved[HEAD:])
        ends = jnp.where(left_lanes, ends[:HEAD], ends[HEAD:])
        for head in range(2):
            moved_part = packed(moved, head).astype(BF16)
            for half in range(2):
                unit_at = pair * 4 + head * 2 + half
                msg[unit_at, 0:32] = moved_part
                msg[unit_at, 32:48] = packed(ends[half * 32 : half * 32 + 32], head).astype(BF16)


def local_terms(pair, aik, uw, vv, srd, local, start_map):
    solved = two_heads(uw[pair])
    scores = aik[pair]
    read = dot(scores[:, : 2 * ROWS], solved)
    keyed = dot(scores[:, 2 * ROWS :], two_heads(vv[pair]))
    local[pair] = read[:, :PAIR] + keyed
    start_map[pair] = (srd[pair] + read[:, PAIR:]).astype(BF16)


def scanned(n_seq, backward, recv, ret, inside):
    def place(i):
        return i + backward * (n_seq - 1 - 2 * i)

    size = 4
    groups = n_seq // size
    left = left_half((HEAD + 32, PAIR))
    blank = jnp.zeros((HEAD, PAIR), BF16)

    def block(i):
        value = recv[place(i)].astype(F32)
        whole = jnp.concatenate([unpacked(value[:32]), unpacked(value[32:])], axis=0)
        return jnp.where(left, whole, 0.0)

    def through(state, mapping):
        full = jnp.concatenate([mapping.astype(BF16), blank], axis=0)
        return dot(state.astype(BF16), full)

    for k in range(size):
        for g in range(groups):
            new = block(g * size + k)
            if k:
                so_far = inside[g * size + k - 1]
                new = so_far + new + through(so_far, new[:HEAD])
            inside[g * size + k] = new

    def onward(g, state):
        whole = inside[g * size + size - 1]
        for k in range(size):
            here = state
            if k:
                before = inside[g * size + k - 1]
                here = here + before[HEAD:] + through(here, before[:HEAD])
            ret[place(g * size + k)] = packed(here, 0).astype(BF16)

        return state + whole[HEAD:] + through(state, whole[:HEAD])

    lax.fori_loop(0, groups, onward, jnp.zeros((32, PAIR), F32))


def incoming(pair, states):
    rows = []
    left = left_half((16, PAIR))
    for head in range(2):
        for half in range(2):
            value = states[pair * 4 + head * 2 + half].astype(F32)
            turned = pltpu.roll(value, HEAD, 1)
            if head == 0:
                rows += [jnp.where(left, value, 0.0), jnp.where(left, turned, 0.0)]
            else:
                rows += [jnp.where(left, 0.0, turned), jnp.where(left, 0.0, value)]
    return jnp.concatenate(rows, axis=0).astype(BF16)


def grouped(pair, states, local, start_map, ones):
    out = local[pair] + dot_t(start_map[pair], incoming(pair, states))
    high, low = halves(out)
    centered = out - (dot(high, ones) + dot(low, ones)) * (1.0 / HEAD)
    spread = dot((centered * centered).astype(BF16), ones) * (1.0 / HEAD)
    return centered * lax.rsqrt(spread + GROUP_EPS)


def kernel(
    n_seq, n_mp,
    ids_in, hidden_fwd, hidden_rc, embed, gain1_in, gain2_in, mix_in,
    w_r, w_k, w_v, d_first_in, d_base_in, d_second_in, c_first_in, i_base_in, c_second_in,
    group_gain_in, w_out, ffn_key, ffn_value,
    out,
    ids, gain1, gain2, mix, d_first, d_base, d_second, c_first, i_base, c_second, group_gain,
    wr, wk, wv, fk, fv, wo,
    xf, xr, embf, prev, nxt, ids_prev, ids_next,
    st, nrm, mx, proj, masks, msg, recv, ret, states, aik, uw, vv, srd, local, start_map,
    joined, residual, act, part, got, inside,
    lsem, ss1, rs1, ss2, rs2, ss3, rs3, ss4, rs4,
):
    j, m = lax.axis_index("seq"), lax.axis_index("mp")

    def seq_at(offset):
        return lax.rem(j + offset + n_seq, n_seq)

    def mp_at(offset):
        return lax.rem(m + offset, n_mp)

    def send(src, dst, sems, index, device):
        copy = pltpu.make_async_remote_copy(
            src_ref=src, dst_ref=dst, send_sem=sems[0].at[index], recv_sem=sems[1].at[index],
            device_id=device, device_id_type=MESH,
        )
        copy.start()
        return copy

    def edge_act(act_remote, act_local):
        for up in (True, False):
            rows, place, seq_to = (0, prev, above) if up else (ROWS - 16, nxt, below)
            source, target = hidden_rc.at[pl.ds(rows, 16)], place.at[1, m]

            def remote(k, index=20 if up else 24, source=source, target=target, seq_to=seq_to):
                act_remote(
                    pltpu.make_async_remote_copy(
                        src_ref=source, dst_ref=target,
                        send_sem=ss1.at[index + k], recv_sem=rs1.at[index + k],
                        device_id=(seq_to, mp_at(k)), device_id_type=MESH,
                    )
                )

            pl.when(seq_to != j)(functools.partial(remote, 0))
            for k in range(1, n_mp):
                remote(k)
            if act_local is not None:

                @pl.when(seq_to == j)
                def _(source=source, target=target, sem=lsem.at[21 + int(up)]):
                    act_local(pltpu.make_async_copy(source, target, sem))

    def fetch(src, dst, index):
        copy = pltpu.make_async_copy(src, dst, lsem.at[index])
        copy.start()
        return copy

    barrier = pltpu.get_barrier_semaphore()

    above, below = lax.rem(n_seq - j, n_seq), lax.rem(2 * n_seq - 2 - j, n_seq)

    def greet(seq_to, mp_to):
        pl.semaphore_signal(barrier, inc=1, device_id=(seq_to, mp_to), device_id_type=MESH)

    for k in range(1, n_mp):
        greet(j, mp_at(k))
        greet(seq_at(1), mp_at(k))
        greet(seq_at(-1), mp_at(k))
        greet(above, mp_at(k))
        greet(below, mp_at(k))

    def greet_far(d, carry):
        greet(seq_at(d), m)
        return carry

    lax.fori_loop(1, n_seq, greet_far, None)
    greet(n_seq - 1 - j, mp_at(2))
    greet(j + 4 - 8 * lax.rem(j // 4, 2), mp_at(2))

    weights = [
        fetch(src, dst, i)
        for i, (src, dst) in enumerate(
            [(w_r, wr), (w_k, wk), (w_v, wv), (ffn_key, fk), (ffn_value, fv)]
        )
    ]
    own = [
        fetch(src, dst, 5 + i)
        for i, (src, dst) in enumerate(
            [
                (hidden_fwd, xf.at[m]), (embed, embf.at[m]), (ids_in, ids), (gain1_in, gain1),
                (mix_in, mix), (d_first_in, d_first), (d_base_in, d_base),
                (d_second_in, d_second), (c_first_in, c_first), (i_base_in, i_base),
                (c_second_in, c_second), (gain2_in, gain2), (group_gain_in, group_gain),
                (w_out, wo.at[m]),
            ]
        )
    ]
    masks_into(masks)
    pl.semaphore_wait(barrier, 5 * (n_mp - 1) + n_seq + 1)

    one = (ss1, rs1)
    copies = {}
    sibling = m + 1 - 2 * lax.rem(m, 2)
    across = mp_at(2)
    mirrored = n_seq - 1 - j
    flipped = j + 4 - 8 * lax.rem(j // 4, 2)
    copies["fwd", 1] = send(hidden_fwd, xf.at[m], one, 1, (j, across))
    copies["fwd", 0] = send(hidden_fwd, xf.at[m], one, 0, (j, sibling))
    for k in range(n_mp):
        copies["f_up", k] = send(
            hidden_fwd.at[pl.ds(ROWS - 16, 16)], prev.at[0, m], one, 6 + k, (seq_at(1), mp_at(k))
        )
        copies["f_down", k] = send(
            hidden_fwd.at[pl.ds(0, 16)], nxt.at[0, m], one, 10 + k, (seq_at(-1), mp_at(k))
        )
    copies["i_up"] = send(ids_in, ids_prev, one, 14, (seq_at(1), m))
    copies["i_down"] = send(ids_in, ids_next, one, 15, (seq_at(-1), m))
    for k in range(1, n_mp):
        copies["emb", k] = send(embed, embf.at[m], one, 2 + k, (j, mp_at(k)))
    edge_act(lambda copy: copy.start(), lambda copy: copy.start())
    copies["rc", 0] = send(hidden_rc, xr.at[m], one, 16, (mirrored, m))
    copies["rc", 1] = send(hidden_rc, xr.at[m], one, 17, (mirrored, across))

    has_prev = (j > 0).astype(F32)
    has_next = (j < n_seq - 1).astype(F32)

    def edges(b):
        sign, base = (1.0, 0.0) if b == 0 else (-1.0, 3.0)
        before = base + sign * ids_prev[0:1, ROWS - 1 : ROWS].astype(F32)
        after = base + sign * ids_next[0:1, 0:1].astype(F32)
        last, first = (15, 0) if b == 0 else (0, 15)
        gain = gain1[...]
        nrm[7:8] = edge_row(prev.at[b], last, before, embf, gain, has_prev)
        nrm[136:137] = edge_row(nxt.at[b], first, after, embf, gain, has_next)

    def strand(b):
        projected(mx, wr, wk, wv, d_first, d_base, d_second, c_first, i_base, c_second, proj)
        block_terms(b, proj, masks, msg, aik, uw, vv, srd)

    def to_unit(d):
        return pltpu.make_async_remote_copy(
            src_ref=msg.at[seq_at(d)], dst_ref=recv.at[j],
            send_sem=ss2.at[d], recv_sem=rs2.at[d],
            device_id=(seq_at(d), m), device_id_type=MESH,
        )

    def to_block(d):
        return pltpu.make_async_remote_copy(
            src_ref=ret.at[seq_at(d)], dst_ref=states.at[j],
            send_sem=ss3.at[d], recv_sem=rs3.at[d],
            device_id=(seq_at(d), m), device_id_type=MESH,
        )

    def each(action):
        def body(d, carry):
            action(d)
            return carry

        lax.fori_loop(1, n_seq, body, None)

    def give_units(b):
        def start(d):
            @pl.when(lax.rem(seq_at(d) // 8, 2) == b)
            def _():
                to_unit(d).start()

        each(start)

    copies["fwd", 1].wait_recv()
    copies["fwd", 2] = send(xf.at[across], xf.at[across], one, 2, (j, sibling))
    for copy in own:
        copy.wait()
    letters = jnp.transpose(jnp.broadcast_to(ids[...].astype(F32), (ROWS, ROWS)))
    for k in range(1, n_mp):
        copies["emb", k].wait_recv()
    copies["fwd", 0].wait_recv()
    copies["fwd", 2].wait_recv()
    for k in range(n_mp):
        copies["f_up", k].wait_recv()
        copies["f_down", k].wait_recv()
    copies["i_up"].wait_recv()
    copies["i_down"].wait_recv()
    strand_rows(
        0, lambda t: xf[t // 2, :, (t % 2) * PAIR : (t % 2 + 1) * PAIR].astype(F32),
        letters, embf, st,
    )
    edges(0)
    normed_and_mixed(0, st, nrm, mx, gain1[...], mix)

    copies["rc", 0].wait_recv()
    copies["rc", 2] = send(xr.at[m], xr.at[m], one, 18, (j, sibling))
    copies["rc", 1].wait_recv()
    copies["rc", 3] = send(xr.at[across], xr.at[across], one, 19, (j, sibling))
    copies["w_near"] = send(w_out, wo.at[m], one, 28, (j, sibling))
    for index, seq_to in enumerate((j, flipped)):
        rows = pl.ds(index * ROWS, ROWS)
        copies["w_far", index] = send(
            w_out.at[rows], wo.at[m, rows], one, 29 + 2 * index, (seq_to, across)
        )
    for copy in weights[:3]:
        copy.wait()
    strand(0)
    give_units(0)

    copies["rc", 2].wait_recv()
    copies["rc", 3].wait_recv()
    edge_act(lambda copy: copy.wait_recv(), lambda copy: copy.wait())
    turn = jnp.where(
        iota2((ROWS, ROWS), 0) + iota2((ROWS, ROWS), 1) == ROWS - 1, 1.0, 0.0
    ).astype(BF16)
    strand_rows(
        1, lambda t: dot(turn, xr[t // 2, :, (t % 2) * PAIR : (t % 2 + 1) * PAIR]),
        3.0 - letters, embf, st,
    )
    edges(1)
    normed_and_mixed(1, st, nrm, mx, gain1[...], mix)
    strand(1)

    give_units(1)
    own_msg = fetch(msg.at[j], recv.at[j], 19)

    def local_body(pair, carry):
        local_terms(pair, aik, uw, vv, srd, local, start_map)
        return carry

    lax.fori_loop(0, 8, local_body, None)
    copies["w_far", 0].wait_recv()
    copies["w_far", 1].wait_recv()
    copies["w_on"] = send(wo.at[across], wo.at[across], one, 30, (j, sibling))
    own_msg.wait()
    each(lambda d: to_unit(d).wait_recv())
    scanned(n_seq, j // (n_seq // 2), recv, ret, inside)
    each(lambda d: to_block(d).start())
    own_ret = fetch(ret.at[j], states.at[j], 20)
    own_ret.wait()
    each(lambda d: to_block(d).wait_recv())

    same_head = iota2((PAIR, PAIR), 0) // HEAD == iota2((PAIR, PAIR), 1) // HEAD
    ones = jnp.where(same_head, 1.0, 0.0).astype(BF16)
    four = (ss4, rs4)
    for b in range(2):
        for q in range(2):
            total = grouped(b * 2 + q, states, local, start_map, ones) + grouped(
                4 + b * 2 + q, states, local, start_map, ones
            )
            lanes = slice(q * PAIR, (q + 1) * PAIR)
            joined[m, b * ROWS : (b + 1) * ROWS, lanes] = (
                total * group_gain[:, lanes]
            ).astype(BF16)
        block = joined.at[m, pl.ds(b * ROWS, ROWS)]
        copies["join", b, 1] = send(block, block, four, b * 3 + 1, (j, across))
        copies["join", b, 0] = send(block, block, four, b * 3, (j, sibling))
    for b in range(2):
        block = joined.at[across, pl.ds(b * ROWS, ROWS)]
        copies["join", b, 1].wait_recv()
        copies["join", b, 2] = send(block, block, four, b * 3 + 2, (j, sibling))

    copies["w_near"].wait_recv()
    copies["w_on"].wait_recv()
    for copy in weights[3:]:
        copy.wait()
    for b in range(2):
        copies["join", b, 0].wait_recv()
        copies["join", b, 2].wait_recv()
        rows = slice(b * ROWS, (b + 1) * ROWS)
        whole = st[b].astype(F32)
        for s in range(n_mp):
            whole = whole + dot(joined[s, rows], wo[s])
        residual[rows] = whole
        ffn_in = layer_norm(whole, gain2[...]).astype(BF16)
        act[rows] = jnp.square(jnp.maximum(dot(ffn_in, fk[...]), 0.0)).astype(BF16)

    def partial(index):
        lanes = pl.ds(pl.multiple_of(index * 2 * PAIR, PAIR), 2 * PAIR)
        both = dot(act[...], fv[:, lanes])
        return both[:ROWS] + both[ROWS:], lanes

    for k, peer in enumerate((across, lax.rem(sibling + 2, n_mp), sibling)):
        value, _ = partial(peer)
        part[k] = value.astype(BF16)
        copies["sum", k] = send(part.at[k], got.at[k], four, 6 + k, (j, peer))
    value, lanes = partial(m)
    value = value + residual[:ROWS, lanes] + residual[ROWS:, lanes]
    for k in (2, 0, 1):
        copies["sum", k].wait_recv()
        value = value + got[k].astype(F32)
    out[...] = value.astype(BF16)

    for copy in copies.values():
        copy.wait_send()
    edge_act(lambda copy: copy.wait_send(), None)
    each(lambda d: to_unit(d).wait_send())
    each(lambda d: to_block(d).wait_send())


def on_device(n_seq, n_mp, *args):
    args = list(args)
    args[0] = args[0].reshape(1, ROWS)
    for index in (4, 5, 11, 14, 16):
        args[index] = args[index].reshape(1, -1)
    for index in (10, 13):
        args[index] = args[index].T
    vmem = pltpu.VMEM
    dma = pltpu.SemaphoreType.DMA
    width = 2 * PAIR
    scratch = [
        vmem((1, ROWS), jnp.int32), vmem((1, 1024), F32), vmem((1, 1024), F32),
        vmem((5, 1024), F32), vmem((64, 1024), BF16), vmem((1, width), F32),
        vmem((64, width), BF16), vmem((64, 1024), BF16), vmem((1, width), F32),
        vmem((64, width), BF16), vmem((1, width), F32),
        vmem((1024, width), BF16), vmem((1024, width), BF16), vmem((1024, width), BF16),
        vmem((1024, 1024), BF16), vmem((1024, 1024), BF16), vmem((n_mp, width, 1024), BF16),
        vmem((n_mp, ROWS, width), BF16), vmem((n_mp, ROWS, width), BF16),
        vmem((n_mp, 4, width), F32),
        vmem((2, n_mp, 16, width), BF16), vmem((2, n_mp, 16, width), BF16),
        vmem((1, ROWS), jnp.int32), vmem((1, ROWS), jnp.int32),
        vmem((2, ROWS, 1024), BF16), vmem((144, 1024), F32), vmem((5, 2 * ROWS, 1024), BF16),
        vmem((7, 2, 2, ROWS, PAIR), F32), vmem((2, LEVELS, ROWS, ROWS), BF16),
        vmem((32, 48, PAIR), BF16), vmem((n_seq, 48, PAIR), BF16),
        vmem((n_seq, 16, PAIR), BF16), vmem((32, 16, PAIR), BF16),
        vmem((8, ROWS, 4 * ROWS), BF16), vmem((8, ROWS, width), BF16),
        vmem((8, ROWS, PAIR), BF16), vmem((8, ROWS, PAIR), F32),
        vmem((8, ROWS, PAIR), F32), vmem((8, ROWS, PAIR), BF16),
        vmem((n_mp, 2 * ROWS, width), BF16), vmem((2 * ROWS, 1024), F32),
        vmem((2 * ROWS, 1024), BF16), vmem((3, ROWS, width), BF16), vmem((3, ROWS, width), BF16),
        vmem((n_seq, 96, PAIR), F32),
        dma((23,)), dma((32,)), dma((32,)), dma((n_seq,)), dma((n_seq,)),
        dma((n_seq,)), dma((n_seq,)), dma((9,)), dma((9,)),
    ]
    return pl.pallas_call(
        functools.partial(kernel, n_seq, n_mp),
        out_shape=jax.ShapeDtypeStruct((ROWS, width), BF16),
        in_specs=[
            pl.BlockSpec(memory_space=pl.ANY)
            for _ in args
        ],
        out_specs=pl.BlockSpec(memory_space=pltpu.VMEM),
        scratch_shapes=scratch,
        compiler_params=pltpu.CompilerParams(
            collective_id=0, has_side_effects=True, vmem_limit_bytes=60 * 1024 * 1024
        ),
    )(*args)


def solution(mesh):
    seq, split, rows = P("seq", "mp"), P(None, "mp"), P("mp", None)
    vec, all_ = P("mp"), P()
    placed = (
        P("seq"), seq, seq, split, all_, all_, all_, split, split, split,
        all_, vec, split, all_, vec, split, vec, rows, split, rows,
    )
    return jax.shard_map(
        functools.partial(on_device, mesh.shape["seq"], mesh.shape["mp"]),
        mesh=mesh, in_specs=placed, out_specs=seq, check_vma=False,
    )
```

```python
import functools

import jax
import jax.numpy as jnp
from jax import lax
from jax.experimental import pallas as pl
from jax.experimental.pallas import tpu as pltpu
from jax.sharding import PartitionSpec as P

F32, BF16 = jnp.float32, jnp.bfloat16
HEAD = 64
ROWS = 128
PAIR = 128
LEVELS = 7
DECAY_SCALE = 0.606531
NORM_EPS = 1e-05
GROUP_EPS = 0.00064
UNIT_EPS = 1e-06
MESH = pl.DeviceIdType.MESH


def dot(a, b):
    return lax.dot_general(a, b, (((1,), (0,)), ((), ())), preferred_element_type=F32)


def dot_t(a, b):
    return lax.dot_general(a, b, (((1,), (1,)), ((), ())), preferred_element_type=F32)


def t_dot(a, b):
    return lax.dot_general(a, b, (((0,), (0,)), ((), ())), preferred_element_type=F32)


def halves(value):
    high = value.astype(BF16)
    return high, (value - high.astype(F32)).astype(BF16)


def iota2(shape, dim):
    return lax.broadcasted_iota(jnp.int32, shape, dim)


def left_half(shape):
    return iota2(shape, 1) % PAIR < HEAD


def layer_norm(values, gain):
    centered = values - jnp.mean(values, axis=-1, keepdims=True)
    spread = jnp.mean(centered * centered, axis=-1, keepdims=True)
    return centered * lax.rsqrt(spread + NORM_EPS) * gain


def masks_into(masks):
    row, col = iota2((ROWS, ROWS), 0), iota2((ROWS, ROWS), 1)
    for level in range(LEVELS):
        size = 1 << level
        same = row // (2 * size) == col // (2 * size)
        row_odd, col_odd = (row // size) % 2, (col // size) % 2
        masks[0, level] = jnp.where(same & (row_odd > col_odd), 1.0, 0.0).astype(BF16)
        masks[1, level] = jnp.where(same & (row_odd < col_odd), 1.0, 0.0).astype(BF16)


def two_heads(value):
    left = left_half(value.shape)
    zero = jnp.zeros_like(value)
    return jnp.concatenate([jnp.where(left, value, zero), jnp.where(left, zero, value)], axis=0)


def on_diagonal(first, second):
    zero = jnp.zeros_like(first)
    upper = jnp.concatenate([first, zero], axis=1)
    return jnp.concatenate([upper, jnp.concatenate([zero, second], axis=1)], axis=0)


def packed(value, head):
    half = value.shape[0] // 2
    upper, lower = value[:half], value[half:]
    left = left_half(upper.shape)
    if head == 0:
        return jnp.where(left, upper, pltpu.roll(lower, HEAD, 1))
    return jnp.where(left, pltpu.roll(upper, HEAD, 1), lower)


def unpacked(value):
    return jnp.concatenate([value, pltpu.roll(value, HEAD, 1)], axis=0)


def strand_rows(b, x_tile, idm, embf, st):
    for tile in range(8):
        slot, lanes = tile // 2, pl.ds((tile % 2) * PAIR, PAIR)
        added = embf[slot, 3:4, lanes]
        for letter in range(3):
            added = jnp.where(idm == float(letter), embf[slot, letter : letter + 1, lanes], added)
        st[b, :, tile * PAIR : (tile + 1) * PAIR] = (x_tile(tile) + added).astype(BF16)


def edge_row(piece, index, letter_of, embf, gain, keep):
    row = jnp.concatenate([piece[s].astype(F32)[index : index + 1] for s in range(4)], axis=1)
    letter = jnp.broadcast_to(letter_of, row.shape)
    emb = [jnp.concatenate([embf[s, c : c + 1] for s in range(4)], axis=1) for c in range(4)]
    added = emb[3]
    for c in range(3):
        added = jnp.where(letter == float(c), emb[c], added)
    row = (row + added).astype(BF16).astype(F32)
    return layer_norm(row, gain) * keep


def normed_and_mixed(b, st, nrm, mx, gain, mix):
    for chunk in range(4):
        rows = pl.ds(chunk * 32, 32)
        nrm[8 + chunk * 32 : 40 + chunk * 32] = layer_norm(st[b, rows].astype(F32), gain)
    for chunk in range(8):
        at = chunk * 16
        center = nrm[8 + at : 24 + at]
        before = nrm[7 + at : 23 + at] - center
        after = nrm[9 + at : 25 + at] - center
        for index in range(5):
            weight = mix[index : index + 1, :]
            mx[index, at : at + 16] = (center + before * weight).astype(BF16)
            mx[index, ROWS + at : ROWS + at + 16] = (center + after * weight).astype(BF16)


def projected(mx, wr, wk, wv, dfw, dbase, dsw, cfw, ibase, csw, proj):
    def keep(index, value):
        for beta in range(2):
            for q in range(2):
                proj[index, beta, q] = value[
                    beta * ROWS : (beta + 1) * ROWS, q * PAIR : (q + 1) * PAIR
                ]

    keep(0, dot(mx[0], wr[...]))
    key = dot(mx[1], wk[...])
    keep(1, key)
    keep(2, dot(mx[2], wv[...]))
    width = 2 * PAIR
    same_head = iota2((width, width), 0) // HEAD == iota2((width, width), 1) // HEAD
    ones = jnp.where(same_head, 1.0, 0.0).astype(BF16)
    high, low = halves(key * key)
    square = dot(high, ones) + dot(low, ones)
    keep(3, key * lax.rsqrt(square + UNIT_EPS))
    low_iclr = dot_t(mx[4], cfw[...]).astype(BF16)
    keep(4, jax.nn.sigmoid(ibase[...] + dot(low_iclr, csw[...])))
    low_decay = jnp.tanh(dot_t(mx[3], dfw[...])).astype(BF16)
    log_decay = -DECAY_SCALE * jax.nn.sigmoid(dbase[...] + dot(low_decay, dsw[...]))
    keep(5, log_decay)
    row, col = iota2((ROWS, ROWS), 0), iota2((ROWS, ROWS), 1)
    totals = []
    for beta in range(2):
        passed = (row >= col) if beta == 0 else (row <= col)
        ones = jnp.where(passed, 1.0, 0.0).astype(BF16)
        high, low = halves(log_decay[beta * ROWS : (beta + 1) * ROWS])
        totals.append(dot(ones, high) + dot(ones, low))
    keep(6, jnp.concatenate(totals, axis=0))


def block_terms(b, proj, masks, msg, aik, uw, vv, srd):
    row, col = iota2((ROWS, ROWS), 0), iota2((ROWS, ROWS), 1)
    eye = jnp.where(row == col, 1.0, 0.0).astype(BF16)
    chains, later = [], []
    for beta in range(2):
        strict = (row > col) if beta == 0 else (row < col)
        inclusive = (row >= col) if beta == 0 else (row <= col)
        for q in range(2):
            pair = (beta * 2 + b) * 2 + q
            receptance, key, value, unit, iclr, log_decay, total = [
                proj[i, beta, q] for i in range(7)
            ]
            middle = total[64:65] if beta == 0 else total[63:64]
            final = total[127:128] if beta == 0 else total[0:1]
            scale_right = jnp.exp(middle - total)
            left_prev = -unit * jnp.exp(total - log_decay - middle)
            left_here = receptance * jnp.exp(total - middle)
            right_insert = iclr * unit * scale_right
            right_key = key * scale_right
            from_start = jnp.exp(middle)
            to_end = jnp.exp(final - middle)
            left = jnp.concatenate(
                [two_heads(left_prev.astype(BF16)), two_heads(left_here.astype(BF16))], axis=0
            )
            right = jnp.concatenate([right_insert, right_key], axis=0).astype(BF16)
            scores = dot_t(left, right)
            pulls, lowers = [], []
            for head in range(2):
                at = head * ROWS
                lower = jnp.where(strict, scores[at : at + ROWS, :ROWS], 0.0).astype(BF16)
                lowers.append(lower)
                pulls.append(jnp.where(strict, scores[at : at + ROWS, ROWS:], 0.0).astype(BF16))
                read = 2 * ROWS + at
                aik[pair, :, at : at + ROWS] = jnp.where(
                    inclusive, scores[read : read + ROWS, :ROWS], 0.0
                ).astype(BF16)
                aik[pair, :, 2 * ROWS + at : 3 * ROWS + at] = jnp.where(
                    inclusive, scores[read : read + ROWS, ROWS:], 0.0
                ).astype(BF16)
            inverse = jnp.concatenate([eye + lower * masks[beta, 0] for lower in lowers], axis=1)
            chains.append([beta, lowers, inverse])
            value = value.astype(BF16)
            vv[pair] = value
            srd[pair] = left_here * from_start
            pulled = dot(jnp.concatenate(pulls, axis=1), two_heads(value))
            wanted = jnp.concatenate([pulled, left_prev * from_start], axis=1).astype(BF16)
            tail_insert = (right_insert * to_end).astype(BF16)
            tail_key = (right_key * to_end).astype(BF16)
            later.append((pair, wanted, value, tail_insert, tail_key, final))
    for level in range(1, LEVELS):
        size = 1 << level
        steps = []
        for beta, lowers, inverse in chains:
            if size >= 16:
                starts = range(0 if beta else size, ROWS, 2 * size)
                inverse = jnp.concatenate([inverse[at : at + size] for at in starts], axis=0)
            level_mask = masks[beta, level]
            below = on_diagonal(*[lower * level_mask for lower in lowers])
            steps.append(dot(inverse, below).astype(BF16))
        for chain, step in zip(chains, steps):
            beta, _, inverse = chain
            step = dot(step, on_diagonal(inverse[:, :ROWS], inverse[:, ROWS:])).astype(BF16)
            if size >= 16:
                blocks = [inverse[at : at + size] for at in range(0, ROWS, size)]
                for index in range(ROWS // (2 * size)):
                    changed = 2 * index + 1 - beta
                    blocks[changed] = blocks[changed] + step[index * size : (index + 1) * size]
                chain[2] = jnp.concatenate(blocks, axis=0)
            else:
                chain[2] = inverse + step
    left_lanes = left_half((HEAD, PAIR))
    for index, (pair, wanted, value, tail_insert, tail_key, final) in enumerate(later):
        solved = dot(chains[index][2], two_heads(wanted)).astype(BF16)
        uw[pair] = solved
        both = t_dot(solved, tail_insert)
        ends = both[:PAIR] + t_dot(value, tail_key)
        moved = both[PAIR:] + jnp.where(row == col, jnp.exp(final) - 1.0, 0.0)
        moved = jnp.where(left_lanes, moved[:HEAD], moved[HEAD:])
        ends = jnp.where(left_lanes, ends[:HEAD], ends[HEAD:])
        for head in range(2):
            moved_part = packed(moved, head).astype(BF16)
            for half in range(2):
                unit_at = pair * 4 + head * 2 + half
                msg[unit_at, 0:32] = moved_part
                msg[unit_at, 32:48] = packed(ends[half * 32 : half * 32 + 32], head).astype(BF16)


def local_terms(pair, aik, uw, vv, srd, local, start_map):
    solved = two_heads(uw[pair])
    scores = aik[pair]
    read = dot(scores[:, : 2 * ROWS], solved)
    keyed = dot(scores[:, 2 * ROWS :], two_heads(vv[pair]))
    local[pair] = read[:, :PAIR] + keyed
    start_map[pair] = (srd[pair] + read[:, PAIR:]).astype(BF16)


def scanned(n_seq, backward, recv, ret, inside, arrive):
    def place(i):
        return i + backward * (n_seq - 1 - 2 * i)

    size = 4
    groups = n_seq // size
    left = left_half((HEAD + 32, PAIR))
    blank = jnp.zeros((HEAD, PAIR), BF16)

    def block(i):
        value = recv[place(i)].astype(F32)
        whole = jnp.concatenate([unpacked(value[:32]), unpacked(value[32:])], axis=0)
        return jnp.where(left, whole, 0.0)

    def through(state, mapping):
        full = jnp.concatenate([mapping.astype(BF16), blank], axis=0)
        return dot(state.astype(BF16), full)

    def combine(first, last):
        for k in range(size):
            for g in range(first, last):
                new = block(g * size + k)
                if k:
                    so_far = inside[g * size + k - 1]
                    new = so_far + new + through(so_far, new[:HEAD])
                inside[g * size + k] = new

    def onward(g, state):
        whole = inside[g * size + size - 1]
        for k in range(size):
            here = state
            if k:
                before = inside[g * size + k - 1]
                here = here + before[HEAD:] + through(here, before[:HEAD])
            ret[place(g * size + k)] = packed(here, 0).astype(BF16)

        return state + whole[HEAD:] + through(state, whole[:HEAD])

    half = groups // 2
    arrive(True)
    combine(0, half)
    state = lax.fori_loop(0, half, onward, jnp.zeros((32, PAIR), F32))
    arrive(False)
    combine(half, groups)
    lax.fori_loop(half, groups, onward, state)


def incoming(pair, states):
    rows = []
    left = left_half((16, PAIR))
    for head in range(2):
        for half in range(2):
            value = states[pair * 4 + head * 2 + half].astype(F32)
            turned = pltpu.roll(value, HEAD, 1)
            if head == 0:
                rows += [jnp.where(left, value, 0.0), jnp.where(left, turned, 0.0)]
            else:
                rows += [jnp.where(left, 0.0, turned), jnp.where(left, 0.0, value)]
    return jnp.concatenate(rows, axis=0).astype(BF16)


def grouped(pair, states, local, start_map, ones):
    out = local[pair] + dot_t(start_map[pair], incoming(pair, states))
    high, low = halves(out)
    centered = out - (dot(high, ones) + dot(low, ones)) * (1.0 / HEAD)
    spread = dot((centered * centered).astype(BF16), ones) * (1.0 / HEAD)
    return centered * lax.rsqrt(spread + GROUP_EPS)


def kernel(
    n_seq, n_mp,
    ids_in, hidden_fwd, hidden_rc, embed, gain1_in, gain2_in, mix_in,
    w_r, w_k, w_v, d_first_in, d_base_in, d_second_in, c_first_in, i_base_in, c_second_in,
    group_gain_in, w_out, ffn_key, ffn_value,
    out,
    ids, gain1, gain2, mix, d_first, d_base, d_second, c_first, i_base, c_second, group_gain,
    wr, wk, wv, fk, fv, wo,
    xf, xr, embf, prev, nxt, ids_prev, ids_next,
    st, nrm, mx, proj, masks, msg, recv, ret, states, aik, uw, vv, srd, local, start_map,
    joined, residual, act, part, got, inside,
    lsem, ss1, rs1, ss2, rs2, ss3, rs3, ss4, rs4,
):
    j, m = lax.axis_index("seq"), lax.axis_index("mp")

    def seq_at(offset):
        return lax.rem(j + offset + n_seq, n_seq)

    def mp_at(offset):
        return lax.rem(m + offset, n_mp)

    def send(src, dst, sems, index, device):
        copy = pltpu.make_async_remote_copy(
            src_ref=src, dst_ref=dst, send_sem=sems[0].at[index], recv_sem=sems[1].at[index],
            device_id=device, device_id_type=MESH,
        )
        copy.start()
        return copy

    def edge_act(act_remote, act_local):
        for up in (True, False):
            rows, place, seq_to = (0, prev, above) if up else (ROWS - 16, nxt, below)
            source, target = hidden_rc.at[pl.ds(rows, 16)], place.at[1, m]

            def remote(k, index=20 if up else 24, source=source, target=target, seq_to=seq_to):
                act_remote(
                    pltpu.make_async_remote_copy(
                        src_ref=source, dst_ref=target,
                        send_sem=ss1.at[index + k], recv_sem=rs1.at[index + k],
                        device_id=(seq_to, mp_at(k)), device_id_type=MESH,
                    )
                )

            pl.when(seq_to != j)(functools.partial(remote, 0))
            for k in range(1, n_mp):
                remote(k)
            if act_local is not None:

                @pl.when(seq_to == j)
                def _(source=source, target=target, sem=lsem.at[21 + int(up)]):
                    act_local(pltpu.make_async_copy(source, target, sem))

    def fetch(src, dst, index):
        copy = pltpu.make_async_copy(src, dst, lsem.at[index])
        copy.start()
        return copy

    barrier = pltpu.get_barrier_semaphore()

    above, below = lax.rem(n_seq - j, n_seq), lax.rem(2 * n_seq - 2 - j, n_seq)

    def greet(seq_to, mp_to):
        pl.semaphore_signal(barrier, inc=1, device_id=(seq_to, mp_to), device_id_type=MESH)

    for k in range(1, n_mp):
        greet(j, mp_at(k))
        greet(seq_at(1), mp_at(k))
        greet(seq_at(-1), mp_at(k))
        greet(above, mp_at(k))
        greet(below, mp_at(k))

    def greet_far(d, carry):
        greet(seq_at(d), m)
        return carry

    lax.fori_loop(1, n_seq, greet_far, None)
    greet(n_seq - 1 - j, mp_at(2))
    greet(j + 4 - 8 * lax.rem(j // 4, 2), mp_at(2))

    weights = [
        fetch(src, dst, i)
        for i, (src, dst) in enumerate(
            [(w_r, wr), (w_k, wk), (w_v, wv), (ffn_key, fk), (ffn_value, fv)]
        )
    ]
    own = [
        fetch(src, dst, 5 + i)
        for i, (src, dst) in enumerate(
            [
                (hidden_fwd, xf.at[m]), (embed, embf.at[m]), (ids_in, ids), (gain1_in, gain1),
                (mix_in, mix), (d_first_in, d_first), (d_base_in, d_base),
                (d_second_in, d_second), (c_first_in, c_first), (i_base_in, i_base),
                (c_second_in, c_second), (gain2_in, gain2), (group_gain_in, group_gain),
                (w_out, wo.at[m]),
            ]
        )
    ]
    masks_into(masks)
    pl.semaphore_wait(barrier, 5 * (n_mp - 1) + n_seq + 1)

    one = (ss1, rs1)
    copies = {}
    sibling = m + 1 - 2 * lax.rem(m, 2)
    across = mp_at(2)
    mirrored = n_seq - 1 - j
    flipped = j + 4 - 8 * lax.rem(j // 4, 2)
    copies["fwd", 1] = send(hidden_fwd, xf.at[m], one, 1, (j, across))
    copies["fwd", 0] = send(hidden_fwd, xf.at[m], one, 0, (j, sibling))
    for k in range(n_mp):
        copies["f_up", k] = send(
            hidden_fwd.at[pl.ds(ROWS - 16, 16)], prev.at[0, m], one, 6 + k, (seq_at(1), mp_at(k))
        )
        copies["f_down", k] = send(
            hidden_fwd.at[pl.ds(0, 16)], nxt.at[0, m], one, 10 + k, (seq_at(-1), mp_at(k))
        )
    copies["i_up"] = send(ids_in, ids_prev, one, 14, (seq_at(1), m))
    copies["i_down"] = send(ids_in, ids_next, one, 15, (seq_at(-1), m))
    for k in range(1, n_mp):
        copies["emb", k] = send(embed, embf.at[m], one, 2 + k, (j, mp_at(k)))
    edge_act(lambda copy: copy.start(), lambda copy: copy.start())
    copies["rc", 0] = send(hidden_rc, xr.at[m], one, 16, (mirrored, m))
    copies["rc", 1] = send(hidden_rc, xr.at[m], one, 17, (mirrored, across))

    has_prev = (j > 0).astype(F32)
    has_next = (j < n_seq - 1).astype(F32)

    def edges(b):
        sign, base = (1.0, 0.0) if b == 0 else (-1.0, 3.0)
        before = base + sign * ids_prev[0:1, ROWS - 1 : ROWS].astype(F32)
        after = base + sign * ids_next[0:1, 0:1].astype(F32)
        last, first = (15, 0) if b == 0 else (0, 15)
        gain = gain1[...]
        nrm[7:8] = edge_row(prev.at[b], last, before, embf, gain, has_prev)
        nrm[136:137] = edge_row(nxt.at[b], first, after, embf, gain, has_next)

    def strand(b):
        projected(mx, wr, wk, wv, d_first, d_base, d_second, c_first, i_base, c_second, proj)
        block_terms(b, proj, masks, msg, aik, uw, vv, srd)

    def to_unit(d):
        return pltpu.make_async_remote_copy(
            src_ref=msg.at[seq_at(d)], dst_ref=recv.at[j],
            send_sem=ss2.at[d], recv_sem=rs2.at[d],
            device_id=(seq_at(d), m), device_id_type=MESH,
        )

    def to_block(d):
        return pltpu.make_async_remote_copy(
            src_ref=ret.at[seq_at(d)], dst_ref=states.at[j],
            send_sem=ss3.at[d], recv_sem=rs3.at[d],
            device_id=(seq_at(d), m), device_id_type=MESH,
        )

    def each(action):
        def body(d, carry):
            action(d)
            return carry

        lax.fori_loop(1, n_seq, body, None)

    def give_units(b):
        def start(d):
            @pl.when(lax.rem(seq_at(d) // 8, 2) == b)
            def _():
                to_unit(d).start()

        each(start)

    copies["fwd", 1].wait_recv()
    copies["fwd", 2] = send(xf.at[across], xf.at[across], one, 2, (j, sibling))
    for copy in own:
        copy.wait()
    letters = jnp.transpose(jnp.broadcast_to(ids[...].astype(F32), (ROWS, ROWS)))
    for k in range(1, n_mp):
        copies["emb", k].wait_recv()
    copies["fwd", 0].wait_recv()
    copies["fwd", 2].wait_recv()
    for k in range(n_mp):
        copies["f_up", k].wait_recv()
        copies["f_down", k].wait_recv()
    copies["i_up"].wait_recv()
    copies["i_down"].wait_recv()
    strand_rows(
        0, lambda t: xf[t // 2, :, (t % 2) * PAIR : (t % 2 + 1) * PAIR].astype(F32),
        letters, embf, st,
    )
    edges(0)
    normed_and_mixed(0, st, nrm, mx, gain1[...], mix)

    copies["rc", 0].wait_recv()
    copies["rc", 2] = send(xr.at[m], xr.at[m], one, 18, (j, sibling))
    copies["rc", 1].wait_recv()
    copies["rc", 3] = send(xr.at[across], xr.at[across], one, 19, (j, sibling))
    copies["w_near"] = send(w_out, wo.at[m], one, 28, (j, sibling))
    for index, seq_to in enumerate((j, flipped)):
        rows = pl.ds(index * ROWS, ROWS)
        copies["w_far", index] = send(
            w_out.at[rows], wo.at[m, rows], one, 29 + 2 * index, (seq_to, across)
        )
    for copy in weights[:3]:
        copy.wait()
    strand(0)
    give_units(0)

    copies["rc", 2].wait_recv()
    copies["rc", 3].wait_recv()
    edge_act(lambda copy: copy.wait_recv(), lambda copy: copy.wait())
    turn = jnp.where(
        iota2((ROWS, ROWS), 0) + iota2((ROWS, ROWS), 1) == ROWS - 1, 1.0, 0.0
    ).astype(BF16)
    strand_rows(
        1, lambda t: dot(turn, xr[t // 2, :, (t % 2) * PAIR : (t % 2 + 1) * PAIR]),
        3.0 - letters, embf, st,
    )
    edges(1)
    normed_and_mixed(1, st, nrm, mx, gain1[...], mix)
    strand(1)

    give_units(1)
    own_msg = fetch(msg.at[j], recv.at[j], 19)

    def local_body(pair, carry):
        local_terms(pair, aik, uw, vv, srd, local, start_map)
        return carry

    lax.fori_loop(0, 8, local_body, None)
    copies["w_far", 0].wait_recv()
    copies["w_far", 1].wait_recv()
    copies["w_on"] = send(wo.at[across], wo.at[across], one, 30, (j, sibling))
    own_msg.wait()

    def arrive(near):
        def wait(d):
            apart = lax.rem(seq_at(-d) // (n_seq // 2) + j // (n_seq // 2), 2)

            @pl.when(apart == int(not near))
            def _():
                to_unit(d).wait_recv()

        each(wait)

    scanned(n_seq, j // (n_seq // 2), recv, ret, inside, arrive)
    each(lambda d: to_block(d).start())
    own_ret = fetch(ret.at[j], states.at[j], 20)
    own_ret.wait()
    each(lambda d: to_block(d).wait_recv())

    same_head = iota2((PAIR, PAIR), 0) // HEAD == iota2((PAIR, PAIR), 1) // HEAD
    ones = jnp.where(same_head, 1.0, 0.0).astype(BF16)
    four = (ss4, rs4)
    for b in range(2):
        for q in range(2):
            total = grouped(b * 2 + q, states, local, start_map, ones) + grouped(
                4 + b * 2 + q, states, local, start_map, ones
            )
            lanes = slice(q * PAIR, (q + 1) * PAIR)
            joined[m, b * ROWS : (b + 1) * ROWS, lanes] = (
                total * group_gain[:, lanes]
            ).astype(BF16)
        block = joined.at[m, pl.ds(b * ROWS, ROWS)]
        copies["join", b, 1] = send(block, block, four, b * 3 + 1, (j, across))
        copies["join", b, 0] = send(block, block, four, b * 3, (j, sibling))
    for b in range(2):
        block = joined.at[across, pl.ds(b * ROWS, ROWS)]
        copies["join", b, 1].wait_recv()
        copies["join", b, 2] = send(block, block, four, b * 3 + 2, (j, sibling))

    copies["w_near"].wait_recv()
    copies["w_on"].wait_recv()
    for copy in weights[3:]:
        copy.wait()
    for b in range(2):
        copies["join", b, 0].wait_recv()
        copies["join", b, 2].wait_recv()
        rows = slice(b * ROWS, (b + 1) * ROWS)
        whole = st[b].astype(F32)
        for s in range(n_mp):
            whole = whole + dot(joined[s, rows], wo[s])
        residual[rows] = whole
        ffn_in = layer_norm(whole, gain2[...]).astype(BF16)
        act[rows] = jnp.square(jnp.maximum(dot(ffn_in, fk[...]), 0.0)).astype(BF16)

    def partial(index):
        lanes = pl.ds(pl.multiple_of(index * 2 * PAIR, PAIR), 2 * PAIR)
        both = dot(act[...], fv[:, lanes])
        return both[:ROWS] + both[ROWS:], lanes

    for k, peer in enumerate((across, lax.rem(sibling + 2, n_mp), sibling)):
        value, _ = partial(peer)
        part[k] = value.astype(BF16)
        copies["sum", k] = send(part.at[k], got.at[k], four, 6 + k, (j, peer))
    value, lanes = partial(m)
    value = value + residual[:ROWS, lanes] + residual[ROWS:, lanes]
    for k in (2, 0, 1):
        copies["sum", k].wait_recv()
        value = value + got[k].astype(F32)
    out[...] = value.astype(BF16)

    for copy in copies.values():
        copy.wait_send()
    edge_act(lambda copy: copy.wait_send(), None)
    each(lambda d: to_unit(d).wait_send())
    each(lambda d: to_block(d).wait_send())


def on_device(n_seq, n_mp, *args):
    args = list(args)
    args[0] = args[0].reshape(1, ROWS)
    for index in (4, 5, 11, 14, 16):
        args[index] = args[index].reshape(1, -1)
    for index in (10, 13):
        args[index] = args[index].T
    vmem = pltpu.VMEM
    dma = pltpu.SemaphoreType.DMA
    width = 2 * PAIR
    scratch = [
        vmem((1, ROWS), jnp.int32), vmem((1, 1024), F32), vmem((1, 1024), F32),
        vmem((5, 1024), F32), vmem((64, 1024), BF16), vmem((1, width), F32),
        vmem((64, width), BF16), vmem((64, 1024), BF16), vmem((1, width), F32),
        vmem((64, width), BF16), vmem((1, width), F32),
        vmem((1024, width), BF16), vmem((1024, width), BF16), vmem((1024, width), BF16),
        vmem((1024, 1024), BF16), vmem((1024, 1024), BF16), vmem((n_mp, width, 1024), BF16),
        vmem((n_mp, ROWS, width), BF16), vmem((n_mp, ROWS, width), BF16),
        vmem((n_mp, 4, width), F32),
        vmem((2, n_mp, 16, width), BF16), vmem((2, n_mp, 16, width), BF16),
        vmem((1, ROWS), jnp.int32), vmem((1, ROWS), jnp.int32),
        vmem((2, ROWS, 1024), BF16), vmem((144, 1024), F32), vmem((5, 2 * ROWS, 1024), BF16),
        vmem((7, 2, 2, ROWS, PAIR), F32), vmem((2, LEVELS, ROWS, ROWS), BF16),
        vmem((32, 48, PAIR), BF16), vmem((n_seq, 48, PAIR), BF16),
        vmem((n_seq, 16, PAIR), BF16), vmem((32, 16, PAIR), BF16),
        vmem((8, ROWS, 4 * ROWS), BF16), vmem((8, ROWS, width), BF16),
        vmem((8, ROWS, PAIR), BF16), vmem((8, ROWS, PAIR), F32),
        vmem((8, ROWS, PAIR), F32), vmem((8, ROWS, PAIR), BF16),
        vmem((n_mp, 2 * ROWS, width), BF16), vmem((2 * ROWS, 1024), F32),
        vmem((2 * ROWS, 1024), BF16), vmem((3, ROWS, width), BF16), vmem((3, ROWS, width), BF16),
        vmem((n_seq, 96, PAIR), F32),
        dma((23,)), dma((32,)), dma((32,)), dma((n_seq,)), dma((n_seq,)),
        dma((n_seq,)), dma((n_seq,)), dma((9,)), dma((9,)),
    ]
    return pl.pallas_call(
        functools.partial(kernel, n_seq, n_mp),
        out_shape=jax.ShapeDtypeStruct((ROWS, width), BF16),
        in_specs=[
            pl.BlockSpec(memory_space=pl.ANY)
            for _ in args
        ],
        out_specs=pl.BlockSpec(memory_space=pltpu.VMEM),
        scratch_shapes=scratch,
        compiler_params=pltpu.CompilerParams(
            collective_id=0, has_side_effects=True, vmem_limit_bytes=60 * 1024 * 1024
        ),
    )(*args)


def solution(mesh):
    seq, split, rows = P("seq", "mp"), P(None, "mp"), P("mp", None)
    vec, all_ = P("mp"), P()
    placed = (
        P("seq"), seq, seq, split, all_, all_, all_, split, split, split,
        all_, vec, split, all_, vec, split, vec, rows, split, rows,
    )
    return jax.shard_map(
        functools.partial(on_device, mesh.shape["seq"], mesh.shape["mp"]),
        mesh=mesh, in_specs=placed, out_specs=seq, check_vma=False,
    )
```
